128 devices in a mesh: wide: 32 (over x, z, core), narrow: 4 (over y).
Axes of the slice: x: 4, y: 4, z: 4, core: 2. Of those that a mesh axis runs over, the one named last changes fastest.
Arguments:
- tokens: bfloat16 [262144, 1024], P(('wide', 'narrow')), may hold values from -64 to 64
- slot_params: bfloat16 [1024, 512], replicated, may hold values from -2.5 to 2.5
- expert_in: bfloat16 [128, 1024, 4096], P('wide', None, 'narrow'), may hold values from -0.1875 to 0.1875
- expert_out: bfloat16 [128, 4096, 1024], P('wide', 'narrow'), may hold values from -0.09375 to 0.09375
Outputs:
- mixed: bfloat16 [262144, 1024], P(('wide', 'narrow'))
The draws below stay inside these ranges and needn't reach their ends.
All inputs are finite; a program needn't handle non-finite values.
Results may differ from the reference program's by a relative error of at most 0.0071.
Values may be sent and summed in bfloat16 or wider, within the bound.
A program may use at most 128 MiB of HBM per device.

```python
import math
import jax
import jax.numpy as jnp
from jax import lax

D = 1024
EXPERT_UNITS = 4096
SLOT_PER = 4
EXPERTS = 128
SLOTS = 512
TOKENS = 262144


def slot_table(key):
    table = 3.0 * jax.random.normal(jax.random.fold_in(key, 11), (D, SLOTS), jnp.float32) / math.sqrt(D)
    table = jnp.clip(table, -2.5, 2.5)
    return table.astype(jnp.bfloat16).astype(jnp.float32)


def draw_slot_params(key, part):
    return slot_table(key).astype(jnp.bfloat16)


def draw_tokens(key, part):
    base = jax.random.normal(jax.random.fold_in(key, 12), (TOKENS, D), jnp.float32)
    base = jnp.clip(base, -6.0, 6.0)
    return base.astype(jnp.bfloat16)


def levels(key, extent, cuts, least, high):
    factor_of, own = 1.0, jax.random.fold_in(key, 6)
    for dim, shards_of in cuts:
        heights = jnp.exp(jax.random.uniform(jax.random.fold_in(own, dim), (shards_of,), jnp.float32, least / len(cuts), high / len(cuts)))
        factor_of = factor_of * jnp.repeat(heights, extent[dim] // shards_of).reshape([-1 if axis == dim else 1 for axis in range(len(extent))])
    return factor_of


def centred(rng, dims, width, bound, cuts=(), kind=jnp.bfloat16):
    factor_of = levels(rng, dims, cuts, -0.22, 0.18) if cuts else 1.0
    result = jax.random.normal(rng, dims, jnp.float32) * width * factor_of
    return jnp.minimum(jnp.maximum(result, -bound), bound).astype(kind)


def setup_inputs(seed: int = 0) -> dict:
    streams_of = jax.random.split(jax.random.key(seed), 5)
    tokens = draw_tokens(jax.random.fold_in(streams_of[4], 71), 0)
    slot_params = draw_slot_params(jax.random.fold_in(streams_of[4], 71), 0)
    expert_in = centred(streams_of[2], (EXPERTS, D, EXPERT_UNITS), D ** -0.5, 0.1875, ((0, 32), (2, 4)))
    expert_out = centred(streams_of[3], (EXPERTS, EXPERT_UNITS, D), EXPERT_UNITS ** -0.5, 0.09375, ((0, 32), (1, 4)))
    return {"tokens": tokens, "slot_params": slot_params, "expert_in": expert_in, "expert_out": expert_out}


def block_logits(block_tokens, slot_params):
    return jnp.dot(block_tokens, slot_params, preferred_element_type=jnp.float32)


def reference(tokens, slot_params, expert_in, expert_out):
    block_size = math.gcd(TOKENS, 8192)
    grouped = tokens.reshape(TOKENS // block_size, block_size, D)
    peaks = lax.map(lambda block_tokens: jnp.max(block_logits(block_tokens, slot_params), axis=0), grouped)
    column_peak = jnp.max(peaks, axis=0)

    def gather_step(carry, block_tokens):
        totals, sums = carry
        logits = block_logits(block_tokens, slot_params)
        weights = jnp.exp(logits - column_peak)
        totals = totals + jnp.sum(weights, axis=0)
        sums = sums + lax.dot_general(weights.astype(jnp.bfloat16), block_tokens, (((0,), (0,)), ((), ())), preferred_element_type=jnp.float32)
        return (totals, sums), None

    start_carry = (jnp.zeros((SLOTS,), jnp.float32), jnp.zeros((SLOTS, D), jnp.float32))
    (totals, sums), unused = lax.scan(gather_step, start_carry, grouped)
    slot_in = (sums / totals[:, None]).astype(jnp.bfloat16)
    stacked = slot_in.reshape(EXPERTS, SLOT_PER, D)

    def expert_step(operands):
        slot_rows, first_weight, second_weight = operands
        hidden = jax.nn.gelu(jnp.dot(slot_rows, first_weight, preferred_element_type=jnp.float32)).astype(jnp.bfloat16)
        return jnp.dot(hidden, second_weight, preferred_element_type=jnp.float32)

    outputs = lax.map(expert_step, (stacked, expert_in, expert_out)).reshape(SLOTS, D).astype(jnp.bfloat16)

    def combine_block(block_tokens):
        logits = block_logits(block_tokens, slot_params)
        mixing = jax.nn.softmax(logits, axis=1).astype(jnp.bfloat16)
        return jnp.dot(mixing, outputs, preferred_element_type=jnp.float32).astype(jnp.bfloat16)

    mixed = lax.map(combine_block, grouped).reshape(TOKENS, D)
    return mixed
```

```python
import jax
import jax.numpy as jnp
from jax import lax
from jax.experimental import pallas as pl
from jax.experimental.pallas import tpu as pltpu
from jax.sharding import PartitionSpec as P

MESH = pl.DeviceIdType.MESH
F32, BF16 = jnp.float32, jnp.bfloat16
NX, NZ, NY, NC = 4, 4, 4, 2
XZ = NX * NZ
CHIPS = XZ * NY
ROWS = 16
TOK, D, S, H = 2048, 1024, 512, 1024
COLS = D // NY
TCH = 512
NT = TOK // TCH


def dot(a, b):
    return jnp.dot(a, b, preferred_element_type=F32)


def layer_kernel(
    tok_hbm, par_hbm, win_hbm, wout_hbm, out_hbm,
    tok, par, win, wout, logits, disp_t, comb, sums, part, outb, recv,
    peak_own, peak_other, tot_own, tot_other, stats, stats_recv,
    sin, obuf, orecv, so, stage,
    in_sem, w_sem, peak_s, peak_r, tot_s, tot_r, part_s, part_r,
    sc_s, sc_r, st_s, st_r, sin_s, sin_r, o_s, o_r, ag_s, ag_r, fw_s, fw_r, out_sem,
):
    wide = lax.axis_index("wide")
    y = lax.axis_index("narrow")
    core = wide % NC
    xz = wide // NC
    x, z = xz // NZ, xz % NZ
    me = xz * NY + y

    def where_is(k):
        dx, dz = k // NZ, k % NZ
        return ((x + dx) % NX) * NZ + (z + dz) % NZ

    def device(to_xz, to_y):
        return {"wide": to_xz * NC + core, "narrow": to_y}

    other = {"wide": xz * NC + 1 - core, "narrow": y}

    def tok_copy(i):
        rows = pl.ds(i * TCH, TCH)
        return pltpu.make_async_copy(tok_hbm.at[rows], tok.at[rows], in_sem.at[i])

    par_copy = pltpu.make_async_copy(par_hbm, par, in_sem.at[NT])
    par_copy.start()
    for i in range(NT):
        tok_copy(i).start()

    barrier = pltpu.get_barrier_semaphore()

    def greet(k, carry):
        to_xz, to_y = where_is(k // NY), (y + k % NY) % NY
        pl.semaphore_signal(barrier, inc=1, device_id=device(to_xz, to_y), device_id_type=MESH)
        return carry

    pl.semaphore_signal(barrier, inc=1, device_id=other, device_id_type=MESH)
    lax.fori_loop(1, CHIPS, greet, 0)

    par_copy.wait()

    def logits_step(i, peak):
        tok_copy(i).wait()
        rows = pl.ds(pl.multiple_of(i * TCH, TCH), TCH)
        block = dot(tok[rows, :], par[...])
        logits[rows, :] = block
        return jnp.maximum(peak, jnp.max(block, axis=0, keepdims=True))

    peak = lax.fori_loop(0, NT, logits_step, jnp.full((1, S), -jnp.inf, F32))

    win_copy = pltpu.make_async_copy(win_hbm, win, w_sem.at[0])
    wout_copy = pltpu.make_async_copy(wout_hbm, wout, w_sem.at[1])
    win_copy.start()
    wout_copy.start()

    def remote(src, dst, send, recv_sem, to):
        return pltpu.make_async_remote_copy(
            src_ref=src, dst_ref=dst, send_sem=send, recv_sem=recv_sem,
            device_id=to, device_id_type=MESH,
        )

    peak_own[...] = jnp.broadcast_to(peak, (8, S))
    pl.semaphore_wait(barrier, CHIPS)
    peak_copy = remote(peak_own, peak_other, peak_s, peak_r, other)
    peak_copy.start()

    def soften(i, carry):
        rows = pl.ds(pl.multiple_of(i * 256, 256), 256)
        block = logits[rows, :]
        e = jnp.exp(block - jnp.max(block, axis=1, keepdims=True))
        comb[rows, :] = (e / jnp.sum(e, axis=1, keepdims=True)).astype(BF16)
        return carry

    lax.fori_loop(0, 3, soften, 0)
    peak_copy.wait()
    peak = jnp.maximum(peak, peak_other[0:1, :])

    def weigh(i, total):
        rows = pl.ds(pl.multiple_of(i * 256, 256), 256)
        w = jnp.exp(logits[rows, :] - peak)
        disp_t[:, rows] = jnp.transpose(w).astype(BF16)
        return total + jnp.sum(w, axis=0, keepdims=True)

    total = lax.fori_loop(0, TOK // 256, weigh, jnp.zeros((1, S), F32))
    tot_own[...] = jnp.broadcast_to(total, (8, S))
    tot_copy = remote(tot_own, tot_other, tot_s, tot_r, other)
    tot_copy.start()

    def part_copy(j):
        return remote(sums.at[j, :, 1 - core], part.at[j], part_s.at[j], part_r.at[j], other)

    def matmul_step(j):
        to_y = (y + j) % NY
        cols = pl.ds(pl.multiple_of(to_y * COLS, COLS), COLS)
        block = dot(disp_t[...], tok[:, cols])
        sums[j] = block.astype(BF16).reshape(XZ, NC, ROWS, COLS)
        part_copy(j).start()

    def send_step(j):
        to_y = (y + j) % NY
        part_copy(j).wait()
        outb[j] = (sums[j, :, core].astype(F32) + part[j].astype(F32)).astype(BF16)

        def send(k, carry):
            to_xz = where_is(k)
            remote(outb.at[j, to_xz], recv.at[me], sc_s, sc_r, device(to_xz, to_y)).start()
            remote(
                stats.at[to_xz * NC + core], stats_recv.at[me], st_s, st_r, device(to_xz, to_y)
            ).start()
            return carry

        @pl.when(j == 0)
        def _():
            recv[me] = outb[0, xz]
            stats_recv[me] = stats[xz * NC + core]

        lax.fori_loop(jnp.where(j == 0, 1, 0), XZ, send, 0)

    matmul_step(0)
    tot_copy.wait()
    total = total + tot_other[0:1, :]
    lane = lax.broadcasted_iota(jnp.int32, (S // ROWS, ROWS, 128), 2)
    row = lax.broadcasted_iota(jnp.int32, (S // ROWS, ROWS, 128), 1)
    peak_rows = jnp.transpose(jnp.broadcast_to(peak, (128, S))).reshape(S // ROWS, ROWS, 128)
    tot_rows = jnp.transpose(jnp.broadcast_to(total, (128, S))).reshape(S // ROWS, ROWS, 128)
    packed = jnp.where(lane == row, peak_rows, 0.0) + jnp.where(lane == row + ROWS, tot_rows, 0.0)
    stats[...] = jnp.sum(packed, axis=1, keepdims=True)

    def pipe(j, carry):
        matmul_step(j)
        send_step(j - 1)
        return carry

    lax.fori_loop(1, NY, pipe, 0)
    send_step(NY - 1)

    lax.fori_loop(3, TOK // 256, soften, 0)

    def drain(ref, sem):
        pltpu.make_async_copy(ref, ref, sem).wait()

    drain(stats_recv.at[pl.ds(0, CHIPS - 1)], st_r)
    drain(recv.at[pl.ds(0, CHIPS - 1)], sc_r)

    got = stats_recv[...].reshape(CHIPS, 128)
    top = jnp.max(got, axis=0, keepdims=True)
    factor = jnp.exp(jnp.minimum(got - top, 0.0))
    scaled = factor * pltpu.roll(got, 128 - ROWS, 1)
    turned = jnp.transpose(jnp.concatenate([factor, scaled], axis=0))[0:ROWS, :]
    owned = jnp.sum(turned[:, CHIPS:], axis=1, keepdims=True)
    acc = jnp.zeros((ROWS, COLS), F32)
    for q in range(CHIPS):
        acc = acc + turned[:, q : q + 1] * recv[q].astype(F32)
    sin[y] = (acc / owned).astype(BF16)

    def sin_copy(k):
        return remote(
            sin.at[y], sin.at[y], sin_s.at[k - 1], sin_r.at[k - 1],
            {"wide": wide, "narrow": (y + k) % NY},
        )

    for k in range(1, NY):
        sin_copy(k).start()
    win_copy.wait()
    wout_copy.wait()
    for k in range(1, NY):
        sin_copy(k).wait()

    expert = lax.broadcasted_iota(jnp.int32, (ROWS, H), 0) // 4
    slot_in = jnp.concatenate([sin[n] for n in range(NY)], axis=1)
    hidden = jnp.zeros((ROWS, H), F32)
    for e in range(4):
        hidden = jnp.where(expert == e, dot(slot_in, win[e]), hidden)
    hidden = jax.nn.gelu(hidden).astype(BF16).astype(F32)
    total_out = jnp.zeros((ROWS, D), F32)
    for e in range(4):
        total_out = total_out + dot(jnp.where(expert == e, hidden, 0.0).astype(BF16), wout[e])
    for n in range(NY):
        obuf[n] = total_out[:, n * COLS : (n + 1) * COLS]

    def o_copy(k):
        to_y = (y + k) % NY
        return remote(
            obuf.at[to_y], orecv.at[y], o_s.at[k - 1], o_r.at[k - 1], {"wide": wide, "narrow": to_y}
        )

    for k in range(1, NY):
        o_copy(k).start()
    orecv[y] = obuf[y]
    for k in range(1, NY):
        o_copy(k).wait()
    mine = orecv[0] + orecv[1] + orecv[2] + orecv[3]
    cols = pl.ds(pl.multiple_of(y * COLS, COLS), COLS)
    so[xz, core, :, cols] = mine.astype(BF16)

    def spread(k, carry):
        to_xz, to_y = where_is(k // NY), (y + k % NY) % NY
        block = so.at[xz, core, :, cols]
        remote(block, block, ag_s, ag_r.at[k // (CHIPS // NX)], device(to_xz, to_y)).start()
        return carry


    lax.fori_loop(1, CHIPS, spread, 0)

    def forward(dx):
        fx = (x - dx + NX) % NX
        block = so.at[pl.ds(fx * NZ, NZ), core]
        return remote(block, block, fw_s.at[dx], fw_r.at[dx], other)

    for dx in range(NX):
        n = (CHIPS // NX) - (1 if dx == 0 else 0)
        drain(recv.at[pl.ds(0, n)], ag_r.at[dx])
        forward(dx).start()
    for dx in range(NX):
        forward(dx).wait()

    def out_copy(i):
        rows = pl.ds(pl.multiple_of(i * TCH, TCH), TCH)
        return pltpu.make_async_copy(stage.at[rows], out_hbm.at[rows], out_sem.at[i])

    def mix(i, carry):
        rows = pl.ds(pl.multiple_of(i * TCH, TCH), TCH)
        stage[rows, :] = dot(comb[rows, :], so[...].reshape(S, D)).astype(BF16)
        out_copy(i).start()
        return carry

    lax.fori_loop(0, NT, mix, 0)
    drain(stats_recv.at[pl.ds(0, CHIPS - 1)], st_s)
    drain(recv.at[pl.ds(0, CHIPS - 1)], sc_s)
    drain(recv.at[pl.ds(0, CHIPS - 1)], ag_s)
    for i in range(NT):
        out_copy(i).wait()


def shards(tokens, slot_params, expert_in, expert_out):
    dma, vmem = pltpu.SemaphoreType.DMA, pltpu.VMEM
    return pl.pallas_call(
        layer_kernel,
        out_shape=jax.ShapeDtypeStruct((TOK, D), BF16),
        in_specs=[pl.BlockSpec(memory_space=pl.ANY)] * 4,
        out_specs=pl.BlockSpec(memory_space=pl.ANY),
        scratch_shapes=[
            vmem((TOK, D), BF16),
            vmem((D, S), BF16),
            vmem((4, D, H), BF16),
            vmem((4, H, D), BF16),
            vmem((TOK, S), F32),
            vmem((S, TOK), BF16),
            vmem((TOK, S), BF16),
            vmem((NY, XZ, NC, ROWS, COLS), BF16),
            vmem((NY, XZ, ROWS, COLS), BF16),
            vmem((NY, XZ, ROWS, COLS), BF16),
            vmem((CHIPS, ROWS, COLS), BF16),
            vmem((8, S), F32),
            vmem((8, S), F32),
            vmem((8, S), F32),
            vmem((8, S), F32),
            vmem((S // ROWS, 1, 128), F32),
            vmem((CHIPS, 1, 128), F32),
            vmem((NY, ROWS, COLS), BF16),
            vmem((NY, ROWS, COLS), F32),
            vmem((NY, ROWS, COLS), F32),
            vmem((XZ, NC, ROWS, D), BF16),
            vmem((TOK, D), BF16),
            dma((NT + 1,)),
            dma((2,)),
            dma, dma, dma, dma,
            dma((NY,)), dma((NY,)),
            dma, dma, dma, dma,
            dma((NY - 1,)), dma((NY - 1,)),
            dma((NY - 1,)), dma((NY - 1,)),
            dma, dma((NX,)),
            dma((NX,)), dma((NX,)),
            dma((NT,)),
        ],
        compiler_params=pltpu.CompilerParams(
            collective_id=0, has_side_effects=True, vmem_limit_bytes=60 * 1024 * 1024
        ),
        name="layer",
    )(tokens, slot_params, expert_in, expert_out)


def solution(mesh):
    return jax.shard_map(
        shards,
        mesh=mesh,
        in_specs=(
            P(("wide", "narrow"), None),
            P(),
            P("wide", None, "narrow"),
            P("wide", "narrow", None),
        ),
        out_specs=P(("wide", "narrow"), None),
        check_vma=False,
    )
```

```python
import jax
import jax.numpy as jnp
from jax import lax
from jax.experimental import pallas as pl
from jax.experimental.pallas import tpu as pltpu
from jax.sharding import PartitionSpec as P

MESH = pl.DeviceIdType.MESH
F32, BF16 = jnp.float32, jnp.bfloat16
NX, NZ, NY, NC = 4, 4, 4, 2
XZ = NX * NZ
ROWS = 16
TOK, D, S, H = 2048, 1024, 512, 1024
TCH = 512
NT = TOK // TCH
HALF = D // 2


def dot(a, b):
    return jnp.dot(a, b, preferred_element_type=F32)


def layer_kernel(
    tok_hbm, par_hbm, win_hbm, wout_hbm, out,
    tok, par, win, wout, logits, disp_t, comb, own, give, part, outb, recv,
    core_own, core_other, stats, stats_recv, ybuf, ystat, obuf, so,
    in_sem, w_sem, core_s, core_r, part_s, part_r,
    sc_s, sc_r, st_s, st_r, y_s, y_r, yst_s, yst_r, o_s, o_r, ag_s, ag_r, fw_s, fw_r,
):
    wide = lax.axis_index("wide")
    y = lax.axis_index("narrow")
    core = wide % NC
    xz = wide // NC
    x, z = xz // NZ, xz % NZ

    def where_is(k):
        dx, dz = k // NZ, k % NZ
        return ((x + dx) % NX) * NZ + (z + dz) % NZ

    def device(to_xz):
        return {"wide": to_xz * NC + core, "narrow": y}

    def along_y(k):
        return {"wide": wide, "narrow": (y + k) % NY}

    other = {"wide": xz * NC + 1 - core, "narrow": y}

    def remote(src, dst, send, recv_sem, to):
        return pltpu.make_async_remote_copy(
            src_ref=src, dst_ref=dst, send_sem=send, recv_sem=recv_sem,
            device_id=to, device_id_type=MESH,
        )

    def drain(ref, sem):
        pltpu.make_async_copy(ref, ref, sem).wait()

    def tok_copy(i):
        rows = pl.ds(i * TCH, TCH)
        return pltpu.make_async_copy(tok_hbm.at[rows], tok.at[rows], in_sem.at[i])

    par_copy = pltpu.make_async_copy(par_hbm, par, in_sem.at[NT])
    par_copy.start()
    for i in range(NT):
        tok_copy(i).start()

    barrier = pltpu.get_barrier_semaphore()

    def greet(to):
        pl.semaphore_signal(barrier, inc=1, device_id=to, device_id_type=MESH)

    def greet_plane(k, carry):
        greet(device(where_is(k)))
        return carry

    greet(other)
    for k in range(1, NY):
        greet(along_y(k))
    lax.fori_loop(1, XZ, greet_plane, 0)

    with jax.named_scope("logits"):
        par_copy.wait()

        def logits_step(i, peak):
            tok_copy(i).wait()
            rows = pl.ds(pl.multiple_of(i * TCH, TCH), TCH)
            block = dot(tok[rows, :], par[...])
            logits[rows, :] = block
            return jnp.maximum(peak, jnp.max(block, axis=0, keepdims=True))

        peak = lax.fori_loop(0, NT, logits_step, jnp.full((1, S), -jnp.inf, F32))
        win_copy = pltpu.make_async_copy(win_hbm, win, w_sem.at[0])
        wout_copy = pltpu.make_async_copy(wout_hbm, wout, w_sem.at[1])
        win_copy.start()
        wout_copy.start()

    with jax.named_scope("exps"):

        def weigh(i, total):
            rows = pl.ds(pl.multiple_of(i * 256, 256), 256)
            w = jnp.exp(logits[rows, :] - peak)
            disp_t[:, rows] = jnp.transpose(w).astype(BF16)
            return total + jnp.sum(w, axis=0, keepdims=True)

        total = lax.fori_loop(0, TOK // 256, weigh, jnp.zeros((1, S), F32))
        row8 = lax.broadcasted_iota(jnp.int32, (8, S), 0)
        core_own[...] = jnp.where(row8 == 0, peak, total)

    with jax.named_scope("barrier"):
        pl.semaphore_wait(barrier, XZ - 1 + NY - 1 + 1)
        core_copy = remote(core_own, core_other, core_s, core_r, other)
        core_copy.start()

    def part_copy(c):
        return remote(give.at[c], part.at[c], part_s.at[c], part_r.at[c], other)

    def targets(c):
        return ((x + 1) % NX, (x + 2) % NX) if c == 0 else ((x + 3) % NX, x)

    def matmul_step(c):
        group = S // NX
        lhs = jnp.concatenate(
            [disp_t[pl.ds(pl.multiple_of(tx * group, group), group), :] for tx in targets(c)], axis=0
        )
        block = dot(lhs, tok[...]).reshape(2, NZ, NC, ROWS, D)
        own[c] = jnp.where(core == 0, block[:, :, 0], block[:, :, 1])
        give[c] = jnp.where(core == 0, block[:, :, 1], block[:, :, 0]).astype(BF16)
        part_copy(c).start()

    with jax.named_scope("mm0"):
        matmul_step(0)

    with jax.named_scope("stats"):
        core_copy.wait()
        peak_o, total_o = core_other[0:1, :], core_other[1:2, :]
        chip_peak = jnp.maximum(peak, peak_o)
        f_own, f_other = jnp.exp(peak - chip_peak), jnp.exp(peak_o - chip_peak)
        chip_total = f_own * total + f_other * total_o
        turned = jnp.transpose(
            jnp.concatenate(
                [jnp.broadcast_to(v, (32, S)) for v in (f_own, f_other, chip_peak, chip_total)], axis=0
            )
        ).reshape(S // ROWS, ROWS, 128)
        lane = lax.broadcasted_iota(jnp.int32, (S // ROWS, ROWS, 128), 2)
        row = lax.broadcasted_iota(jnp.int32, (S // ROWS, ROWS, 128), 1)
        packed = jnp.where(lane == row, turned[:, :, 64:65], 0.0)
        packed = packed + jnp.where(lane == row + ROWS, turned[:, :, 96:97], 0.0)
        stats[...] = jnp.sum(packed, axis=1, keepdims=True)
        turned = turned.reshape(NX, NZ, NC, ROWS, 128)
        factors = jnp.where(core == 0, turned[:, :, 0], turned[:, :, 1])
        outb_f = factors

        def send_stats(k, carry):
            to_xz = where_is(k)
            remote(
                stats.at[to_xz * NC + core], stats_recv.at[xz], st_s, st_r, device(to_xz)
            ).start()
            return carry

        lax.fori_loop(1, XZ, send_stats, 0)
        stats_recv[xz] = stats[wide]

    with jax.named_scope("mm1"):
        matmul_step(1)

    def pick(tx):
        f = outb_f[0]
        for n in range(1, NX):
            f = jnp.where(tx == n, outb_f[n], f)
        return f

    def send_step(c):
        part_copy(c).wait()
        for h, tx in enumerate(targets(c)):
            f = pick(tx)
            outb[c, h] = (
                f[:, :, 0:1] * own[c, h] + f[:, :, 32:33] * part[c, h].astype(F32)
            ).astype(BF16)
        for h, tx in enumerate(targets(c)):
            for dz in range(NZ):
                tz = (z + dz) % NZ
                if c == 1 and h == 1 and dz == 0:
                    recv[xz] = outb[c, h, z]
                else:
                    remote(outb.at[c, h, tz], recv.at[xz], sc_s, sc_r, device(tx * NZ + tz)).start()

    def soften(i, carry):
        rows = pl.ds(pl.multiple_of(i * 256, 256), 256)
        block = logits[rows, :]
        e = jnp.exp(block - jnp.max(block, axis=1, keepdims=True))
        comb[rows, :] = (e / jnp.sum(e, axis=1, keepdims=True)).astype(BF16)
        return carry

    with jax.named_scope("send0"):
        send_step(0)
    with jax.named_scope("soft0"):
        lax.fori_loop(0, 3, soften, 0)
    with jax.named_scope("send1"):
        send_step(1)
    with jax.named_scope("soft1"):
        lax.fori_loop(3, TOK // 256, soften, 0)

    with jax.named_scope("scwait"):
        drain(stats_recv.at[pl.ds(0, XZ - 1)], st_r)
        drain(recv.at[pl.ds(0, XZ - 1)], sc_r)

    with jax.named_scope("reduce"):
        got = stats_recv[...].reshape(XZ, 128)
        top = jnp.max(got, axis=0, keepdims=True)
        factor = jnp.exp(jnp.minimum(got - top, 0.0))
        scaled = factor * pltpu.roll(got, 128 - ROWS, 1)
        flipped = jnp.transpose(
            jnp.concatenate([factor, scaled, jnp.broadcast_to(top, (128 - 2 * XZ, 128))], axis=0)
        )[0:ROWS, :]
        acc = jnp.zeros((ROWS, D), F32)
        for q in range(XZ):
            acc = acc + flipped[:, q : q + 1] * recv[q].astype(F32)
        plane_total = jnp.sum(flipped[:, XZ : 2 * XZ], axis=1, keepdims=True)
        ybuf[y] = acc.astype(BF16)
        lane2 = lax.broadcasted_iota(jnp.int32, (ROWS, 128), 1)
        ystat[y] = jnp.where(lane2 < 64, flipped[:, 2 * XZ : 2 * XZ + 1], plane_total)

    def y_copy(k):
        return remote(ybuf.at[y], ybuf.at[y], y_s.at[k - 1], y_r.at[k - 1], along_y(k))

    def ystat_copy(k):
        return remote(ystat.at[y], ystat.at[y], yst_s.at[k - 1], yst_r.at[k - 1], along_y(k))

    with jax.named_scope("yex"):
        for k in (2, 1, 3):
            ystat_copy(k).start()
            y_copy(k).start()
        win_copy.wait()
        wout_copy.wait()
        for k in range(1, NY):
            ystat_copy(k).wait()
            y_copy(k).wait()

    with jax.named_scope("ffn"):
        tops = [ystat[n][:, 0:1] for n in range(NY)]
        gmax = jnp.maximum(jnp.maximum(tops[0], tops[1]), jnp.maximum(tops[2], tops[3]))
        grand = jnp.zeros((ROWS, 1), F32)
        acc = jnp.zeros((ROWS, D), F32)
        for n in range(NY):
            f = jnp.exp(tops[n] - gmax)
            grand = grand + f * ystat[n][:, 64:65]
            acc = acc + f * ybuf[n].astype(F32)
        slot_in = (acc / grand).astype(BF16)
        expert = lax.broadcasted_iota(jnp.int32, (ROWS, H), 0) // 4
        hidden = jnp.zeros((ROWS, H), F32)
        for e in range(4):
            hidden = jnp.where(expert == e, dot(slot_in, win[e]), hidden)
        hidden = jax.nn.gelu(hidden).astype(BF16).astype(F32)
        total_out = jnp.zeros((ROWS, D), F32)
        for e in range(4):
            total_out = total_out + dot(jnp.where(expert == e, hidden, 0.0).astype(BF16), wout[e])
        obuf[y] = total_out

    def o_copy(k):
        return remote(obuf.at[y], obuf.at[y], o_s.at[k - 1], o_r.at[k - 1], along_y(k))

    with jax.named_scope("oex"):
        for k in (2, 1, 3):
            o_copy(k).start()
        for k in range(1, NY):
            o_copy(k).wait()

    def half(h):
        return slice(h * HALF, (h + 1) * HALF)

    def spread(h, k):
        block = so.at[xz, core, :, half(h)]
        return remote(block, block, ag_s, ag_r.at[h, k // NZ], device(where_is(k)))

    def forward(h, dx):
        fx = (x - dx + NX) % NX
        block = so.at[pl.ds(fx * NZ, NZ), core, :, half(h)]
        return remote(block, block, fw_s.at[h, dx], fw_r.at[h, dx], other)

    with jax.named_scope("spread"):
        so[xz, core] = (obuf[0] + obuf[1] + obuf[2] + obuf[3]).astype(BF16)
        for h in range(2):
            for k in range(1, XZ):
                spread(h, k).start()

    for h in range(2):
        with jax.named_scope("agwait"):
            for dx in range(NX):
                n = NZ - (1 if dx == 0 else 0)
                drain(so.at[pl.ds(0, n), 0, :, half(h)], ag_r.at[h, dx])
                forward(h, dx).start()
            for dx in range(NX):
                forward(h, dx).wait()
        with jax.named_scope("mix"):

            def mix(i, carry):
                rows = pl.ds(pl.multiple_of(i * TCH, TCH), TCH)
                table = so[:, :, :, half(h)].reshape(S, HALF)
                out[rows, half(h)] = dot(comb[rows, :], table).astype(BF16)
                return carry

            lax.fori_loop(0, NT, mix, 0)

    drain(stats_recv.at[pl.ds(0, XZ - 1)], st_s)
    drain(recv.at[pl.ds(0, XZ - 1)], sc_s)
    drain(recv.at[pl.ds(0, XZ - 1)], ag_s)


def shards(tokens, slot_params, expert_in, expert_out):
    dma, vmem = pltpu.SemaphoreType.DMA, pltpu.VMEM
    return pl.pallas_call(
        layer_kernel,
        out_shape=pltpu.VMEM((TOK, D), BF16),
        in_specs=[pl.BlockSpec(memory_space=pltpu.HBM)] * 4,
        out_specs=pl.BlockSpec(memory_space=pltpu.VMEM),
        scratch_shapes=[
            vmem((TOK, D), BF16),
            vmem((D, S), BF16),
            vmem((4, D, H), BF16),
            vmem((4, H, D), BF16),
            vmem((TOK, S), F32),
            vmem((S, TOK), BF16),
            vmem((TOK, S), BF16),
            vmem((2, 2, NZ, ROWS, D), F32),
            vmem((2, 2, NZ, ROWS, D), BF16),
            vmem((2, 2, NZ, ROWS, D), BF16),
            vmem((2, 2, NZ, ROWS, D), BF16),
            vmem((XZ, ROWS, D), BF16),
            vmem((8, S), F32),
            vmem((8, S), F32),
            vmem((S // ROWS, 1, 128), F32),
            vmem((XZ, 1, 128), F32),
            vmem((NY, ROWS, D), BF16),
            vmem((NY, ROWS, 128), F32),
            vmem((NY, ROWS, D), F32),
            vmem((XZ, NC, ROWS, D), BF16),
            dma((NT + 1,)),
            dma((2,)),
            dma, dma,
            dma((2,)), dma((2,)),
            dma, dma, dma, dma,
            dma((NY - 1,)), dma((NY - 1,)),
            dma((NY - 1,)), dma((NY - 1,)),
            dma((NY - 1,)), dma((NY - 1,)),
            dma, dma((2, NX)),
            dma((2, NX)), dma((2, NX)),
        ],
        compiler_params=pltpu.CompilerParams(
            collective_id=0, has_side_effects=True, vmem_limit_bytes=50331648
        ),
        name="layer",
    )(*[pltpu.with_memory_space_constraint(v, pltpu.HBM) for v in (tokens, slot_params, expert_in, expert_out)])


def solution(mesh):
    return jax.shard_map(
        shards,
        mesh=mesh,
        in_specs=(
            P(("wide", "narrow"), None),
            P(),
            P("wide", None, "narrow"),
            P("wide", "narrow", None),
        ),
        out_specs=P(("wide", "narrow"), None),
        check_vma=False,
    )
```

```python
import jax
import jax.numpy as jnp
from jax import lax
from jax.experimental import pallas as pl
from jax.experimental.pallas import tpu as pltpu
from jax.sharding import PartitionSpec as P

MESH = pl.DeviceIdType.MESH
F32, BF16 = jnp.float32, jnp.bfloat16
NX, NZ, NY, NC = 4, 4, 4, 2
XZ = NX * NZ
ROWS = 16
PIPE = 2
PR = ROWS // PIPE
TOK, D, S, H = 2048, 1024, 512, 1024
SP = S // PIPE
TCH = 512
NT = TOK // TCH
SOFT = 256


def dot(a, b):
    return jnp.dot(a, b, preferred_element_type=F32)


def layer_kernel(
    tok_hbm, par_hbm, win_hbm, wout_hbm, mixed, comb, last,
    tok, par, win, wout, logits, disp_t, order, own, give, part, outb, recv,
    core_own, core_other, stats, stats_recv, ystat, ybuf, obuf, so, first,
    in_sem, w_sem, core_s, core_r, part_s, part_r, st_s, st_r, sc_s, sc_r,
    yst_s, yst_r, y_s, y_r, o_s, o_r, ag_s, ag_r, fw_s, fw_r,
):
    wide = lax.axis_index("wide")
    y = lax.axis_index("narrow")
    core = wide % NC
    xz = wide // NC
    x, z = xz // NZ, xz % NZ

    def where_is(k):
        dx, dz = k // NZ, k % NZ
        return ((x + dx) % NX) * NZ + (z + dz) % NZ

    def device(to_xz):
        return {"wide": to_xz * NC + core, "narrow": y}

    def along_y(k):
        return {"wide": wide, "narrow": (y + k) % NY}

    other = {"wide": xz * NC + 1 - core, "narrow": y}

    def remote(src, dst, send, recv_sem, to):
        return pltpu.make_async_remote_copy(
            src_ref=src, dst_ref=dst, send_sem=send, recv_sem=recv_sem,
            device_id=to, device_id_type=MESH,
        )

    def drain(ref, sem):
        pltpu.make_async_copy(ref, ref, sem).wait()

    def tok_copy(i):
        rows = pl.ds(i * TCH, TCH)
        return pltpu.make_async_copy(tok_hbm.at[rows], tok.at[rows], in_sem.at[i])

    par_copy = pltpu.make_async_copy(par_hbm, par, in_sem.at[NT])
    par_copy.start()
    tok_copy(0).start()

    barrier = pltpu.get_barrier_semaphore()

    def greet(to):
        pl.semaphore_signal(barrier, inc=1, device_id=to, device_id_type=MESH)

    def greet_plane(k, carry):
        greet(device(where_is(k)))
        return carry

    greet(other)
    for k in range(1, NY):
        greet(along_y(k))
    lax.fori_loop(1, XZ, greet_plane, 0)
    for i in range(1, NT):
        tok_copy(i).start()

    with jax.named_scope("logits"):
        par_copy.wait()

        def logits_step(i, peak):
            tok_copy(i).wait()
            rows = pl.ds(pl.multiple_of(i * TCH, TCH), TCH)
            block = dot(tok[rows, :], par[...])
            logits[rows, :] = block
            return jnp.maximum(peak, jnp.max(block, axis=0, keepdims=True))

        peak = lax.fori_loop(0, NT, logits_step, jnp.full((1, S), -jnp.inf, F32))
        win_copy = pltpu.make_async_copy(win_hbm, win, w_sem.at[0])
        wout_copy = pltpu.make_async_copy(wout_hbm, wout, w_sem.at[1])
        win_copy.start()
        wout_copy.start()

    with jax.named_scope("exps"):

        def weigh(i, total):
            rows = pl.ds(pl.multiple_of(i * 256, 256), 256)
            w = jnp.exp(logits[rows, :] - peak)
            turned = jnp.transpose(w).reshape(S // ROWS, PIPE, PR, 256)
            for p in range(PIPE):
                disp_t[p, :, rows] = turned[:, p].reshape(SP, 256).astype(BF16)
            return total + jnp.sum(w, axis=0, keepdims=True)

        total = lax.fori_loop(0, TOK // 256, weigh, jnp.zeros((1, S), F32))
        row8 = lax.broadcasted_iota(jnp.int32, (8, S), 0)
        core_own[...] = jnp.where(row8 == 0, peak, total)

    with jax.named_scope("barrier"):
        pl.semaphore_wait(barrier, XZ - 1 + NY - 1 + 1)
        core_copy = remote(core_own, core_other, core_s, core_r, other)
        core_copy.start()

    def part_copy(p):
        return remote(give.at[p], part.at[p], part_s.at[p], part_r.at[p], other)

    def matmul_step(p):
        block = dot(disp_t[p], tok[...]).reshape(XZ, NC, PR, D)
        own[p] = jnp.where(core == 0, block[:, 0], block[:, 1])
        give[p] = jnp.where(core == 0, block[:, 1], block[:, 0]).astype(BF16)
        part_copy(p).start()

    with jax.named_scope("mm0"):
        matmul_step(0)

    with jax.named_scope("stats"):
        core_copy.wait()
        peak_o, total_o = core_other[0:1, :], core_other[1:2, :]
        chip_peak = jnp.maximum(peak, peak_o)
        f_own, f_other = jnp.exp(peak - chip_peak), jnp.exp(peak_o - chip_peak)
        chip_total = f_own * total + f_other * total_o
        turned = jnp.transpose(
            jnp.concatenate(
                [jnp.broadcast_to(v, (32, S)) for v in (f_own, f_other, chip_peak, chip_total)], axis=0
            )
        ).reshape(S // ROWS, ROWS, 128)
        lane = lax.broadcasted_iota(jnp.int32, (S // ROWS, ROWS, 128), 2)
        row = lax.broadcasted_iota(jnp.int32, (S // ROWS, ROWS, 128), 1)
        packed = jnp.where(lane == row, turned[:, :, 64:65], 0.0)
        packed = packed + jnp.where(lane == row + ROWS, turned[:, :, 96:97], 0.0)
        stats[...] = jnp.sum(packed, axis=1, keepdims=True)
        turned = turned.reshape(XZ, NC, ROWS, 128)
        factors = jnp.where(core == 0, turned[:, 0], turned[:, 1])

        def send_stats(k, carry):
            to_xz = where_is(k)
            remote(
                stats.at[to_xz * NC + core], stats_recv.at[xz], st_s, st_r, device(to_xz)
            ).start()
            return carry

        lax.fori_loop(1, XZ, send_stats, 0)
        stats_recv[xz] = stats[wide]

    with jax.named_scope("mm1"):
        matmul_step(1)

    def send_step(p):
        part_copy(p).wait()
        f = factors[:, p * PR : (p + 1) * PR]
        outb[p] = (f[:, :, 0:1] * own[p] + f[:, :, 32:33] * part[p].astype(F32)).astype(BF16)

        def send(k, carry):
            to_xz = where_is(k)
            remote(outb.at[p, to_xz], recv.at[p, xz], sc_s.at[p], sc_r.at[p], device(to_xz)).start()
            return carry

        lax.fori_loop(1, XZ, send, 0)
        recv[p, xz] = outb[p, xz]

    def soften(i, carry):
        rows = pl.ds(pl.multiple_of(i * SOFT, SOFT), SOFT)
        block = logits[rows, :]
        e = jnp.exp(block - jnp.max(block, axis=1, keepdims=True))
        share = (e / jnp.sum(e, axis=1, keepdims=True)).astype(BF16)
        comb[rows, :] = dot(share, order[...]).astype(BF16)
        return carry

    with jax.named_scope("send0"):
        send_step(0)
    with jax.named_scope("soft0"):
        new = lax.broadcasted_iota(jnp.int32, (S, S), 1)
        old = lax.broadcasted_iota(jnp.int32, (S, S), 0)
        within = new % SP
        source = (within // PR) * ROWS + (new // SP) * PR + within % PR
        order[...] = jnp.where(old == source, 1.0, 0.0).astype(BF16)
        lax.fori_loop(0, 1, soften, 0)
    with jax.named_scope("send1"):
        send_step(1)
    with jax.named_scope("soft1"):
        lax.fori_loop(1, 5, soften, 0)

    with jax.named_scope("ystat"):
        drain(stats_recv.at[pl.ds(0, XZ - 1)], st_r)
        got = stats_recv[...].reshape(XZ, 128)
        top = jnp.max(got, axis=0, keepdims=True)
        factor = jnp.exp(jnp.minimum(got - top, 0.0))
        scaled = factor * pltpu.roll(got, 128 - ROWS, 1)
        flipped = jnp.transpose(
            jnp.concatenate([factor, scaled, jnp.broadcast_to(top, (128 - 2 * XZ, 128))], axis=0)
        )[0:ROWS, :]
        plane_top = flipped[:, 2 * XZ : 2 * XZ + 1]
        plane_total = jnp.sum(flipped[:, XZ : 2 * XZ], axis=1, keepdims=True)
        lane2 = lax.broadcasted_iota(jnp.int32, (ROWS, 128), 1)
        ystat[y] = jnp.where(lane2 < 64, plane_top, plane_total)

        def ystat_copy(k):
            return remote(ystat.at[y], ystat.at[y], yst_s.at[k - 1], yst_r.at[k - 1], along_y(k))

        for k in (2, 1, 3):
            ystat_copy(k).start()

    with jax.named_scope("soft2"):
        lax.fori_loop(5, TOK // SOFT, soften, 0)

    with jax.named_scope("ystatw"):
        for k in range(1, NY):
            ystat_copy(k).wait()
        tops = [ystat[n][:, 0:1] for n in range(NY)]
        all_top = jnp.maximum(jnp.maximum(tops[0], tops[1]), jnp.maximum(tops[2], tops[3]))
        grand = jnp.zeros((ROWS, 1), F32)
        for n in range(NY):
            grand = grand + jnp.exp(tops[n] - all_top) * ystat[n][:, 64:65]
        scale = jnp.exp(plane_top - all_top) / grand

    def y_copy(p, k):
        return remote(
            ybuf.at[p, y], ybuf.at[p, y], y_s.at[p, k - 1], y_r.at[p, k - 1], along_y(k)
        )

    def o_copy(p, k):
        return remote(
            obuf.at[p, y], obuf.at[p, y], o_s.at[p, k - 1], o_r.at[p, k - 1], along_y(k)
        )

    for p in range(PIPE):
        with jax.named_scope("scwait"):
            drain(recv.at[p, pl.ds(0, XZ - 1)], sc_r.at[p])
        with jax.named_scope("reduce"):
            mine = slice(p * PR, (p + 1) * PR)
            acc = jnp.zeros((PR, D), F32)
            for q in range(XZ):
                acc = acc + flipped[mine, q : q + 1] * recv[p, q].astype(F32)
            ybuf[p, y] = (acc * scale[mine]).astype(BF16)
            for k in (2, 1, 3):
                y_copy(p, k).start()

    win_copy.wait()
    wout_copy.wait()
    per = PR // 4
    expert = lax.broadcasted_iota(jnp.int32, (PR, H), 0) // 4
    for p in range(PIPE):
        with jax.named_scope("yex"):
            for k in range(1, NY):
                y_copy(p, k).wait()
        with jax.named_scope("ffn"):
            slot_in = jnp.sum(ybuf[p].astype(F32), axis=0).astype(BF16)
            hidden = jnp.zeros((PR, H), F32)
            for e in range(per):
                hidden = jnp.where(expert == e, dot(slot_in, win[p * per + e]), hidden)
            hidden = jax.nn.gelu(hidden).astype(BF16).astype(F32)
            result = jnp.zeros((PR, D), F32)
            for e in range(per):
                result = result + dot(
                    jnp.where(expert == e, hidden, 0.0).astype(BF16), wout[p * per + e]
                )
            obuf[p, y] = result
            for k in (2, 1, 3):
                o_copy(p, k).start()

    def spread(p, k):
        block = so.at[p, xz, core]
        return remote(block, block, ag_s.at[p], ag_r.at[p, k // NZ], device(where_is(k)))

    def forward(p, dx):
        fx = (x - dx + NX) % NX
        block = so.at[p, pl.ds(fx * NZ, NZ), core]
        return remote(block, block, fw_s.at[p, dx], fw_r.at[p, dx], other)

    def arrive(p, dx):
        n = NZ - (1 if dx == 0 else 0)
        drain(so.at[p, pl.ds(0, n), 0], ag_r.at[p, dx])
        forward(p, dx).start()

    for p in range(PIPE):
        with jax.named_scope("oex"):
            for k in range(1, NY):
                o_copy(p, k).wait()
        with jax.named_scope("spread"):
            so[p, xz, core] = (obuf[p, 0] + obuf[p, 1] + obuf[p, 2] + obuf[p, 3]).astype(BF16)

            def send_out(k, carry):
                spread(p, k).start()
                return carry

            lax.fori_loop(1, XZ, send_out, 0)

    def mix(i):
        rows = pl.ds(pl.multiple_of(i * TCH, TCH), TCH)
        mixed[rows, :] = dot(comb[rows, 0:SP], first[...])

    with jax.named_scope("agA"):
        for dx in (0, 1, 3, 2):
            arrive(0, dx)
        for dx in range(NX):
            forward(0, dx).wait()
        first[...] = so[0].reshape(SP, D)
    with jax.named_scope("mixA"):
        for i, dx in enumerate((0, 1, 3, 2)):
            mix(i)
            arrive(1, dx)
    with jax.named_scope("agB"):
        for dx in range(NX):
            forward(1, dx).wait()
        last[...] = so[1].reshape(SP, D)

    drain(stats_recv.at[pl.ds(0, XZ - 1)], st_s)
    for p in range(PIPE):
        drain(recv.at[p, pl.ds(0, XZ - 1)], sc_s.at[p])
        drain(recv.at[p, pl.ds(0, XZ - 1)], ag_s.at[p])


def finish_kernel(mixed, comb, last, out, stage, sems):
    def out_copy(i):
        rows = pl.ds(i * SOFT, SOFT)
        return pltpu.make_async_copy(stage.at[rows], out.at[rows], sems.at[i])

    for i in range(TOK // SOFT):
        rows = pl.ds(i * SOFT, SOFT)
        stage[rows, :] = (mixed[rows, :] + dot(comb[rows, SP:S], last[...])).astype(BF16)
        out_copy(i).start()
    for i in range(TOK // SOFT):
        out_copy(i).wait()


def shards(tokens, slot_params, expert_in, expert_out):
    dma, vmem = pltpu.SemaphoreType.DMA, pltpu.VMEM
    operands = [
        pltpu.with_memory_space_constraint(v, pltpu.HBM)
        for v in (tokens, slot_params, expert_in, expert_out)
    ]
    held = pl.pallas_call(
        layer_kernel,
        out_shape=(vmem((TOK, D), F32), vmem((TOK, S), BF16), vmem((SP, D), BF16)),
        in_specs=[pl.BlockSpec(memory_space=pltpu.HBM)] * 4,
        out_specs=[pl.BlockSpec(memory_space=pltpu.VMEM)] * 3,
        scratch_shapes=[
            vmem((TOK, D), BF16),
            vmem((D, S), BF16),
            vmem((4, D, H), BF16),
            vmem((4, H, D), BF16),
            vmem((TOK, S), F32),
            vmem((PIPE, SP, TOK), BF16),
            vmem((S, S), BF16),
            vmem((PIPE, XZ, PR, D), F32),
            vmem((PIPE, XZ, PR, D), BF16),
            vmem((PIPE, XZ, PR, D), BF16),
            vmem((PIPE, XZ, PR, D), BF16),
            vmem((PIPE, XZ, PR, D), BF16),
            vmem((8, S), F32),
            vmem((8, S), F32),
            vmem((S // ROWS, 1, 128), F32),
            vmem((XZ, 1, 128), F32),
            vmem((NY, ROWS, 128), F32),
            vmem((PIPE, NY, PR, D), BF16),
            vmem((PIPE, NY, PR, D), F32),
            vmem((PIPE, XZ, NC, PR, D), BF16),
            vmem((SP, D), BF16),
            dma((NT + 1,)),
            dma((2,)),
            dma, dma,
            dma((PIPE,)), dma((PIPE,)),
            dma, dma,
            dma((PIPE,)), dma((PIPE,)),
            dma((NY - 1,)), dma((NY - 1,)),
            dma((PIPE, NY - 1)), dma((PIPE, NY - 1)),
            dma((PIPE, NY - 1)), dma((PIPE, NY - 1)),
            dma((PIPE,)), dma((PIPE, NX)),
            dma((PIPE, NX)), dma((PIPE, NX)),
        ],
        compiler_params=pltpu.CompilerParams(
            collective_id=0, has_side_effects=True, vmem_limit_bytes=48 * 1024 * 1024
        ),
        name="layer",
    )(*operands)
    return pl.pallas_call(
        finish_kernel,
        out_shape=jax.ShapeDtypeStruct((TOK, D), BF16),
        in_specs=[pl.BlockSpec(memory_space=pltpu.VMEM)] * 3,
        out_specs=pl.BlockSpec(memory_space=pl.ANY),
        scratch_shapes=[vmem((TOK, D), BF16), dma((TOK // SOFT,))],
        compiler_params=pltpu.CompilerParams(vmem_limit_bytes=32 * 1024 * 1024),
        name="finish",
    )(*held)


def solution(mesh):
    return jax.shard_map(
        shards,
        mesh=mesh,
        in_specs=(
            P(("wide", "narrow"), None),
            P(),
            P("wide", None, "narrow"),
            P("wide", "narrow", None),
        ),
        out_specs=P(("wide", "narrow"), None),
        check_vma=False,
    )
```

```python
import jax
import jax.numpy as jnp
from jax import lax
from jax.experimental import pallas as pl
from jax.experimental.pallas import tpu as pltpu
from jax.sharding import PartitionSpec as P

MESH = pl.DeviceIdType.MESH
F32, BF16 = jnp.float32, jnp.bfloat16
NX, NZ, NY, NC = 4, 4, 4, 2
XZ = NX * NZ
ROWS = 16
PIPE = 4
PR = ROWS // PIPE
PH = PIPE // 2
HR = ROWS // 2
TOK, D, S, H = 2048, 1024, 512, 1024
SP = S // PIPE
SH = S // 2
TCH = 512
NT = TOK // TCH
MCH = 512
SOFT = 256


def dot(a, b):
    return jnp.dot(a, b, preferred_element_type=F32)


def layer_kernel(
    tok_hbm, par_hbm, win_hbm, wout_hbm, mixed, comb, last,
    tok, par, win, wout, logits, disp_t, order, own, give, part, outb, recv,
    core_own, core_other, stats, stats_recv, ystat, ybuf, obuf, so, first,
    in_sem, w_sem, core_s, core_r, part_s, part_r, st_s, st_r, sc_s, sc_r,
    yst_s, yst_r, y_s, y_r, o_s, o_r, ag_s, ag_r, fw_s, fw_r,
):
    wide = lax.axis_index("wide")
    y = lax.axis_index("narrow")
    core = wide % NC
    xz = wide // NC
    x, z = xz // NZ, xz % NZ

    def where_is(k):
        dx, dz = k // NZ, k % NZ
        return ((x + dx) % NX) * NZ + (z + dz) % NZ

    def device(to_xz):
        return {"wide": to_xz * NC + core, "narrow": y}

    def along_y(k):
        return {"wide": wide, "narrow": (y + k) % NY}

    other = {"wide": xz * NC + 1 - core, "narrow": y}

    def remote(src, dst, send, recv_sem, to):
        return pltpu.make_async_remote_copy(
            src_ref=src, dst_ref=dst, send_sem=send, recv_sem=recv_sem,
            device_id=to, device_id_type=MESH,
        )

    def drain(ref, sem):
        pltpu.make_async_copy(ref, ref, sem).wait()

    def tok_copy(i):
        rows = pl.ds(i * TCH, TCH)
        return pltpu.make_async_copy(tok_hbm.at[rows], tok.at[rows], in_sem.at[i])

    par_copy = pltpu.make_async_copy(par_hbm, par, in_sem.at[NT])
    par_copy.start()
    tok_copy(0).start()

    barrier = pltpu.get_barrier_semaphore()

    def greet(to):
        pl.semaphore_signal(barrier, inc=1, device_id=to, device_id_type=MESH)

    def greet_plane(k, carry):
        greet(device(where_is(k)))
        return carry

    greet(other)
    for k in range(1, NY):
        greet(along_y(k))
    lax.fori_loop(1, XZ, greet_plane, 0)
    for i in range(1, NT):
        tok_copy(i).start()

    with jax.named_scope("logits"):
        par_copy.wait()

        def logits_step(i, peak):
            tok_copy(i).wait()
            rows = pl.ds(pl.multiple_of(i * TCH, TCH), TCH)
            block = dot(tok[rows, :], par[...])
            logits[rows, :] = block
            return jnp.maximum(peak, jnp.max(block, axis=0, keepdims=True))

        peak = lax.fori_loop(0, NT, logits_step, jnp.full((1, S), -jnp.inf, F32))
        win_copy = pltpu.make_async_copy(win_hbm, win, w_sem.at[0])
        wout_copy = pltpu.make_async_copy(wout_hbm, wout, w_sem.at[1])
        win_copy.start()
        wout_copy.start()

    def weigh(i):
        rows = pl.ds(i * MCH, MCH)
        w = jnp.exp(logits[rows, :] - peak)
        turned = jnp.transpose(w).reshape(S // ROWS, 2, HR, MCH)
        for h in range(2):
            disp_t[h, :, rows] = turned[:, h].reshape(SH, MCH).astype(BF16)
        return jnp.sum(w, axis=0, keepdims=True)

    with jax.named_scope("exps"):
        total = weigh(0)
        block = None
        for i in range(TOK // MCH):
            rows = pl.ds(i * MCH, MCH)
            step = dot(disp_t[0, :, rows], tok[rows, :])
            block = step if block is None else block + step
            if i + 1 < TOK // MCH:
                total = total + weigh(i + 1)
        row8 = lax.broadcasted_iota(jnp.int32, (8, S), 0)
        core_own[...] = jnp.where(row8 == 0, peak, total)

    with jax.named_scope("barrier"):
        pl.semaphore_wait(barrier, XZ - 1 + NY - 1 + 1)
        core_copy = remote(core_own, core_other, core_s, core_r, other)
        core_copy.start()

    def part_copy(h):
        return remote(give.at[h], part.at[h], part_s.at[h], part_r.at[h], other)

    def share_block(h, block):
        block = block.reshape(XZ, NC, HR, D)
        own[h] = jnp.where(core == 0, block[:, 0], block[:, 1])
        give[h] = jnp.where(core == 0, block[:, 1], block[:, 0]).astype(BF16)
        part_copy(h).start()

    with jax.named_scope("mm0"):
        share_block(0, block)

    with jax.named_scope("mm1"):
        share_block(1, dot(disp_t[1], tok[...]))

    with jax.named_scope("stats"):
        core_copy.wait()
        peak_o, total_o = core_other[0:1, :], core_other[1:2, :]
        chip_peak = jnp.maximum(peak, peak_o)
        f_own, f_other = jnp.exp(peak - chip_peak), jnp.exp(peak_o - chip_peak)
        chip_total = f_own * total + f_other * total_o
        turned = jnp.transpose(
            jnp.concatenate(
                [jnp.broadcast_to(v, (32, S)) for v in (f_own, f_other, chip_peak, chip_total)], axis=0
            )
        ).reshape(S // ROWS, ROWS, 128)
        lane = lax.broadcasted_iota(jnp.int32, (S // ROWS, ROWS, 128), 2)
        row = lax.broadcasted_iota(jnp.int32, (S // ROWS, ROWS, 128), 1)
        packed = jnp.where(lane == row, turned[:, :, 64:65], 0.0)
        packed = packed + jnp.where(lane == row + ROWS, turned[:, :, 96:97], 0.0)
        stats[...] = jnp.sum(packed, axis=1, keepdims=True)
        turned = turned.reshape(XZ, NC, ROWS, 128)
        factors = jnp.where(core == 0, turned[:, 0], turned[:, 1])

        def send_stats(k, carry):
            to_xz = where_is(k)
            remote(
                stats.at[to_xz * NC + core], stats_recv.at[xz], st_s, st_r, device(to_xz)
            ).start()
            return carry

        lax.fori_loop(1, XZ, send_stats, 0)
        stats_recv[xz] = stats[wide]

    def send_step(h):
        part_copy(h).wait()
        f = factors[:, h * HR : (h + 1) * HR]
        joined = (f[:, :, 0:1] * own[h] + f[:, :, 32:33] * part[h].astype(F32)).astype(BF16)
        for p in range(h * PH, (h + 1) * PH):
            outb[p] = joined[:, (p % PH) * PR : (p % PH + 1) * PR]
        for p in range(h * PH, (h + 1) * PH):

            def send(k, carry):
                to_xz = where_is(k)
                remote(
                    outb.at[p, to_xz], recv.at[p, xz], sc_s.at[p], sc_r.at[p], device(to_xz)
                ).start()
                return carry

            lax.fori_loop(1, XZ, send, 0)
            recv[p, xz] = outb[p, xz]

    def soften(i, carry):
        rows = pl.ds(pl.multiple_of(i * SOFT, SOFT), SOFT)
        block = logits[rows, :]
        e = jnp.exp(block - jnp.max(block, axis=1, keepdims=True))
        share = (e / jnp.sum(e, axis=1, keepdims=True)).astype(BF16)
        comb[rows, :] = dot(share, order[...]).astype(BF16)
        return carry

    with jax.named_scope("send0"):
        send_step(0)
    with jax.named_scope("soft0"):
        new = lax.broadcasted_iota(jnp.int32, (S, S), 1)
        old = lax.broadcasted_iota(jnp.int32, (S, S), 0)
        within = new % SP
        source = (within // PR) * ROWS + (new // SP) * PR + within % PR
        order[...] = jnp.where(old == source, 1.0, 0.0).astype(BF16)
        lax.fori_loop(0, 1, soften, 0)
    with jax.named_scope("send1"):
        send_step(1)
    with jax.named_scope("soft1"):
        lax.fori_loop(1, 3, soften, 0)

    with jax.named_scope("ystat"):
        drain(stats_recv.at[pl.ds(0, XZ - 1)], st_r)
        got = stats_recv[...].reshape(XZ, 128)
        top = jnp.max(got, axis=0, keepdims=True)
        factor = jnp.exp(jnp.minimum(got - top, 0.0))
        scaled = factor * pltpu.roll(got, 128 - ROWS, 1)
        flipped = jnp.transpose(
            jnp.concatenate([factor, scaled, jnp.broadcast_to(top, (128 - 2 * XZ, 128))], axis=0)
        )[0:ROWS, :]
        plane_top = flipped[:, 2 * XZ : 2 * XZ + 1]
        plane_total = jnp.sum(flipped[:, XZ : 2 * XZ], axis=1, keepdims=True)
        lane2 = lax.broadcasted_iota(jnp.int32, (ROWS, 128), 1)
        ystat[y] = jnp.where(lane2 < 64, plane_top, plane_total)

        def ystat_copy(k):
            return remote(ystat.at[y], ystat.at[y], yst_s.at[k - 1], yst_r.at[k - 1], along_y(k))

        for k in (2, 1, 3):
            ystat_copy(k).start()

    with jax.named_scope("soft2"):
        lax.fori_loop(3, 4, soften, 0)

    def y_copy(p, k):
        return remote(
            ybuf.at[p, y], ybuf.at[p, y], y_s.at[p, k - 1], y_r.at[p, k - 1], along_y(k)
        )

    def o_copy(p, k):
        return remote(
            obuf.at[p, y], obuf.at[p, y], o_s.at[p, k - 1], o_r.at[p, k - 1], along_y(k)
        )

    def gather(p):
        with jax.named_scope(f"sc{p}"):
            drain(recv.at[p, pl.ds(0, XZ - 1)], sc_r.at[p])
            mine = slice(p * PR, (p + 1) * PR)
            acc = jnp.zeros((PR, D), F32)
            for q in range(XZ):
                acc = acc + flipped[mine, q : q + 1] * recv[p, q].astype(F32)
            ybuf[p, y] = acc.astype(BF16)
            for k in (2, 1, 3):
                y_copy(p, k).start()

    def expert(p):
        with jax.named_scope(f"ffn{p}"):
            for k in range(1, NY):
                y_copy(p, k).wait()
            mine = slice(p * PR, (p + 1) * PR)
            acc = jnp.zeros((PR, D), F32)
            for n in range(NY):
                acc = acc + scale[n][mine] * ybuf[p, n].astype(F32)
            hidden = jax.nn.gelu(dot(acc.astype(BF16), win[p])).astype(BF16)
            obuf[p, y] = dot(hidden, wout[p]).astype(BF16)
            for k in (2, 1, 3):
                o_copy(p, k).start()

    def soft(i):
        with jax.named_scope(f"soft{i}"):
            soften(i, 0)

    gather(0)
    gather(1)
    soft(4)
    gather(2)
    with jax.named_scope("ystatw"):
        win_copy.wait()
        wout_copy.wait()
        for k in range(1, NY):
            ystat_copy(k).wait()
        tops = [ystat[n][:, 0:1] for n in range(NY)]
        all_top = jnp.maximum(jnp.maximum(tops[0], tops[1]), jnp.maximum(tops[2], tops[3]))
        scale = [jnp.exp(tops[n] - all_top) for n in range(NY)]
        grand = jnp.zeros((ROWS, 1), F32)
        for n in range(NY):
            grand = grand + scale[n] * ystat[n][:, 64:65]
        scale = [v / grand for v in scale]

    def spread(p, k):
        block = so.at[p, xz, core]
        return remote(block, block, ag_s.at[p], ag_r.at[p, k // NZ], device(where_is(k)))

    def forward(p, dx):
        fx = (x - dx + NX) % NX
        block = so.at[p, pl.ds(fx * NZ, NZ), core]
        return remote(block, block, fw_s.at[p, dx], fw_r.at[p, dx], other)

    def arrive(p, dx):
        n = NZ - (1 if dx == 0 else 0)
        drain(so.at[p, pl.ds(0, n), 0], ag_r.at[p, dx])
        forward(p, dx).start()

    def publish(p):
        with jax.named_scope(f"oex{p}"):
            for k in range(1, NY):
                o_copy(p, k).wait()
            so[p, xz, core] = jnp.sum(obuf[p].astype(F32), axis=0).astype(BF16)

            def send_out(k, carry):
                spread(p, k).start()
                return carry

            lax.fori_loop(1, XZ, send_out, 0)

    expert(0)
    gather(3)
    expert(1)
    soft(5)
    expert(2)
    publish(0)
    expert(3)
    publish(1)
    soft(6)
    publish(2)
    soft(7)
    publish(3)

    def mix(i):
        rows = pl.ds(i * MCH, MCH)
        mixed[rows, :] = dot(comb[rows, 0:SH], first[...])

    turns = (0, 1, 3, 2)
    with jax.named_scope("agA"):
        for p in range(PH):
            for dx in turns:
                arrive(p, dx)
        for p in range(PH):
            for dx in turns:
                forward(p, dx).wait()
        first[...] = so[0:PH].reshape(SH, D)
    with jax.named_scope("mixA"):
        for i, dx in enumerate(turns):
            mix(i)
            if i < 2:
                arrive(2, turns[2 * i])
                arrive(2, turns[2 * i + 1])
            else:
                arrive(3, turns[2 * i - 4])
                arrive(3, turns[2 * i - 3])
    with jax.named_scope("agB"):
        for p in range(PH, PIPE):
            for dx in turns:
                forward(p, dx).wait()
        last[...] = so[PH:PIPE].reshape(SH, D)

    with jax.named_scope("ends"):
        drain(stats_recv.at[pl.ds(0, XZ - 1)], st_s)
        for p in range(PIPE):
            drain(recv.at[p, pl.ds(0, XZ - 1)], sc_s.at[p])
            drain(recv.at[p, pl.ds(0, XZ - 1)], ag_s.at[p])


def finish_kernel(mixed, comb, last, out, stage, sems):
    def out_copy(i):
        rows = pl.ds(i * SOFT, SOFT)
        return pltpu.make_async_copy(stage.at[rows], out.at[rows], sems.at[i])

    for i in range(TOK // SOFT):
        rows = pl.ds(i * SOFT, SOFT)
        stage[rows, :] = (mixed[rows, :] + dot(comb[rows, SH:S], last[...])).astype(BF16)
        out_copy(i).start()
    for i in range(TOK // SOFT):
        out_copy(i).wait()


def shards(tokens, slot_params, expert_in, expert_out):
    dma, vmem = pltpu.SemaphoreType.DMA, pltpu.VMEM
    operands = [
        pltpu.with_memory_space_constraint(v, pltpu.HBM)
        for v in (tokens, slot_params, expert_in, expert_out)
    ]
    held = pl.pallas_call(
        layer_kernel,
        out_shape=(vmem((TOK, D), F32), vmem((TOK, S), BF16), vmem((SH, D), BF16)),
        in_specs=[pl.BlockSpec(memory_space=pltpu.HBM)] * 4,
        out_specs=[pl.BlockSpec(memory_space=pltpu.VMEM)] * 3,
        scratch_shapes=[
            vmem((TOK, D), BF16),
            vmem((D, S), BF16),
            vmem((4, D, H), BF16),
            vmem((4, H, D), BF16),
            vmem((TOK, S), F32),
            vmem((2, SH, TOK), BF16),
            vmem((S, S), BF16),
            vmem((2, XZ, HR, D), F32),
            vmem((2, XZ, HR, D), BF16),
            vmem((2, XZ, HR, D), BF16),
            vmem((PIPE, XZ, PR, D), BF16),
            vmem((PIPE, XZ, PR, D), BF16),
            vmem((8, S), F32),
            vmem((8, S), F32),
            vmem((S // ROWS, 1, 128), F32),
            vmem((XZ, 1, 128), F32),
            vmem((NY, ROWS, 128), F32),
            vmem((PIPE, NY, PR, D), BF16),
            vmem((PIPE, NY, PR, D), BF16),
            vmem((PIPE, XZ, NC, PR, D), BF16),
            vmem((SH, D), BF16),
            dma((NT + 1,)),
            dma((2,)),
            dma, dma,
            dma((2,)), dma((2,)),
            dma, dma,
            dma((PIPE,)), dma((PIPE,)),
            dma((NY - 1,)), dma((NY - 1,)),
            dma((PIPE, NY - 1)), dma((PIPE, NY - 1)),
            dma((PIPE, NY - 1)), dma((PIPE, NY - 1)),
            dma((PIPE,)), dma((PIPE, NX)),
            dma((PIPE, NX)), dma((PIPE, NX)),
        ],
        compiler_params=pltpu.CompilerParams(
            collective_id=0, has_side_effects=True, vmem_limit_bytes=48 * 1024 * 1024
        ),
        name="layer",
    )(*operands)
    return pl.pallas_call(
        finish_kernel,
        out_shape=jax.ShapeDtypeStruct((TOK, D), BF16),
        in_specs=[pl.BlockSpec(memory_space=pltpu.VMEM)] * 3,
        out_specs=pl.BlockSpec(memory_space=pl.ANY),
        scratch_shapes=[vmem((TOK, D), BF16), dma((TOK // SOFT,))],
        compiler_params=pltpu.CompilerParams(vmem_limit_bytes=32 * 1024 * 1024),
        name="finish",
    )(*held)


def solution(mesh):
    return jax.shard_map(
        shards,
        mesh=mesh,
        in_specs=(
            P(("wide", "narrow"), None),
            P(),
            P("wide", None, "narrow"),
            P("wide", "narrow", None),
        ),
        out_specs=P(("wide", "narrow"), None),
        check_vma=False,
    )
```

```python
import jax
import jax.numpy as jnp
from jax import lax
from jax.experimental import pallas as pl
from jax.experimental.pallas import tpu as pltpu
from jax.sharding import PartitionSpec as P

MESH = pl.DeviceIdType.MESH
F32, BF16 = jnp.float32, jnp.bfloat16
NX, NZ, NY, NC = 4, 4, 4, 2
XZ = NX * NZ
ROWS = 16
PIPE = 4
PR = ROWS // PIPE
PH = PIPE // 2
HR = ROWS // 2
TOK, D, S, H = 2048, 1024, 512, 1024
SP = S // PIPE
SH = S // 2
TCH = 512
NT = TOK // TCH
MCH = 512
FAR_FIRST = (10, 9, 6, 11, 14, 5, 7, 13, 15, 8, 2, 4, 1, 12, 3)
SOFT = 256


def dot(a, b):
    return jnp.dot(a, b, preferred_element_type=F32)


def layer_kernel(
    tok_hbm, par_hbm, win_hbm, wout_hbm, mixed, comb, last,
    tok, par, win, wout, logits, disp_t, order, own, give, part, outb, recv,
    core_own, core_other, stats, stats_recv, ystat, ybuf, obuf, so, first,
    in_sem, w_sem, core_s, core_r, part_s, part_r, st_s, st_r, sc_s, sc_r,
    yst_s, yst_r, y_s, y_r, o_s, o_r, ag_s, ag_r, fw_s, fw_r,
):
    wide = lax.axis_index("wide")
    y = lax.axis_index("narrow")
    core = wide % NC
    xz = wide // NC
    x, z = xz // NZ, xz % NZ

    def where_is(k):
        dx, dz = k // NZ, k % NZ
        return ((x + dx) % NX) * NZ + (z + dz) % NZ

    def device(to_xz):
        return {"wide": to_xz * NC + core, "narrow": y}

    def along_y(k):
        return {"wide": wide, "narrow": (y + k) % NY}

    other = {"wide": xz * NC + 1 - core, "narrow": y}

    def remote(src, dst, send, recv_sem, to):
        return pltpu.make_async_remote_copy(
            src_ref=src, dst_ref=dst, send_sem=send, recv_sem=recv_sem,
            device_id=to, device_id_type=MESH,
        )

    def drain(ref, sem):
        pltpu.make_async_copy(ref, ref, sem).wait()

    def tok_copy(i):
        rows = pl.ds(i * TCH, TCH)
        return pltpu.make_async_copy(tok_hbm.at[rows], tok.at[rows], in_sem.at[i])

    par_copy = pltpu.make_async_copy(par_hbm, par, in_sem.at[NT])
    par_copy.start()
    tok_copy(0).start()

    barrier = pltpu.get_barrier_semaphore()

    def greet(to):
        pl.semaphore_signal(barrier, inc=1, device_id=to, device_id_type=MESH)

    greet(other)
    for k in range(1, NY):
        greet(along_y(k))
    for k in range(1, XZ):
        greet(device(where_is(k)))
    for i in range(1, NT):
        tok_copy(i).start()

    with jax.named_scope("logits"):
        par_copy.wait()

        def logits_step(i, peak):
            tok_copy(i).wait()
            rows = pl.ds(pl.multiple_of(i * TCH, TCH), TCH)
            block = dot(tok[rows, :], par[...])
            logits[rows, :] = block
            return jnp.maximum(peak, jnp.max(block, axis=0, keepdims=True))

        peak = lax.fori_loop(0, NT, logits_step, jnp.full((1, S), -jnp.inf, F32))
        win_copy = pltpu.make_async_copy(win_hbm, win, w_sem.at[0])
        wout_copy = pltpu.make_async_copy(wout_hbm, wout, w_sem.at[1])
        win_copy.start()
        wout_copy.start()

    def weigh(i):
        rows = pl.ds(i * MCH, MCH)
        w = jnp.exp(logits[rows, :] - peak)
        turned = jnp.transpose(w).reshape(S // ROWS, 2, HR, MCH)
        for h in range(2):
            disp_t[h, :, rows] = turned[:, h].reshape(SH, MCH).astype(BF16)
        return jnp.sum(w, axis=0, keepdims=True)

    with jax.named_scope("exps"):
        total = weigh(0)
        block = None
        for i in range(TOK // MCH):
            rows = pl.ds(i * MCH, MCH)
            step = dot(disp_t[0, :, rows], tok[rows, :])
            block = step if block is None else block + step
            if i + 1 < TOK // MCH:
                total = total + weigh(i + 1)
        row8 = lax.broadcasted_iota(jnp.int32, (8, S), 0)
        core_own[...] = jnp.where(row8 == 0, peak, total)

    with jax.named_scope("barrier"):
        pl.semaphore_wait(barrier, XZ - 1 + NY - 1 + 1)
        core_copy = remote(core_own, core_other, core_s, core_r, other)
        core_copy.start()

    def part_copy(h):
        return remote(give.at[h], part.at[h], part_s.at[h], part_r.at[h], other)

    def share_block(h, block):
        block = block.reshape(XZ, NC, HR, D)
        own[h] = jnp.where(core == 0, block[:, 0], block[:, 1])
        give[h] = jnp.where(core == 0, block[:, 1], block[:, 0]).astype(BF16)
        part_copy(h).start()

    with jax.named_scope("mm0"):
        share_block(0, block)

    with jax.named_scope("mm1"):
        share_block(1, dot(disp_t[1], tok[...]))

    with jax.named_scope("stats"):
        core_copy.wait()
        peak_o, total_o = core_other[0:1, :], core_other[1:2, :]
        chip_peak = jnp.maximum(peak, peak_o)
        f_own, f_other = jnp.exp(peak - chip_peak), jnp.exp(peak_o - chip_peak)
        chip_total = f_own * total + f_other * total_o
        turned = jnp.transpose(
            jnp.concatenate(
                [jnp.broadcast_to(v, (32, S)) for v in (f_own, f_other, chip_peak, chip_total)], axis=0
            )
        ).reshape(S // ROWS, ROWS, 128)
        lane = lax.broadcasted_iota(jnp.int32, (S // ROWS, ROWS, 128), 2)
        row = lax.broadcasted_iota(jnp.int32, (S // ROWS, ROWS, 128), 1)
        packed = jnp.where(lane == row, turned[:, :, 64:65], 0.0)
        packed = packed + jnp.where(lane == row + ROWS, turned[:, :, 96:97], 0.0)
        stats[...] = jnp.sum(packed, axis=1, keepdims=True)
        turned = turned.reshape(XZ, NC, ROWS, 128)
        factors = jnp.where(core == 0, turned[:, 0], turned[:, 1])

        for k in FAR_FIRST:
            to_xz = where_is(k)
            remote(
                stats.at[to_xz * NC + core], stats_recv.at[xz], st_s, st_r, device(to_xz)
            ).start()
        stats_recv[xz] = stats[wide]

    def send_step(h):
        part_copy(h).wait()
        f = factors[:, h * HR : (h + 1) * HR]
        joined = (f[:, :, 0:1] * own[h] + f[:, :, 32:33] * part[h].astype(F32)).astype(BF16)
        for p in range(h * PH, (h + 1) * PH):
            outb[p] = joined[:, (p % PH) * PR : (p % PH + 1) * PR]
        for p in range(h * PH, (h + 1) * PH):
            for k in FAR_FIRST:
                to_xz = where_is(k)
                remote(
                    outb.at[p, to_xz], recv.at[p, xz], sc_s, sc_r.at[p], device(to_xz)
                ).start()
            recv[p, xz] = outb[p, xz]

    def soften(i, carry):
        rows = pl.ds(pl.multiple_of(i * SOFT, SOFT), SOFT)
        block = logits[rows, :]
        e = jnp.exp(block - jnp.max(block, axis=1, keepdims=True))
        share = (e / jnp.sum(e, axis=1, keepdims=True)).astype(BF16)
        comb[rows, :] = dot(share, order[...]).astype(BF16)
        return carry

    with jax.named_scope("send0"):
        send_step(0)
    with jax.named_scope("send1"):
        send_step(1)
    with jax.named_scope("order"):
        new = lax.broadcasted_iota(jnp.int32, (S, S), 1)
        old = lax.broadcasted_iota(jnp.int32, (S, S), 0)
        within = new % SP
        source = (within // PR) * ROWS + (new // SP) * PR + within % PR
        order[...] = jnp.where(old == source, 1.0, 0.0).astype(BF16)
    with jax.named_scope("soft1"):
        lax.fori_loop(0, 3, soften, 0)

    with jax.named_scope("ystat"):
        drain(stats_recv.at[pl.ds(0, XZ - 1)], st_r)
        got = stats_recv[...].reshape(XZ, 128)
        top = jnp.max(got, axis=0, keepdims=True)
        factor = jnp.exp(jnp.minimum(got - top, 0.0))
        scaled = factor * pltpu.roll(got, 128 - ROWS, 1)
        flipped = jnp.transpose(
            jnp.concatenate([factor, scaled, jnp.broadcast_to(top, (128 - 2 * XZ, 128))], axis=0)
        )[0:ROWS, :]
        plane_top = flipped[:, 2 * XZ : 2 * XZ + 1]
        plane_total = jnp.sum(flipped[:, XZ : 2 * XZ], axis=1, keepdims=True)
        lane2 = lax.broadcasted_iota(jnp.int32, (ROWS, 128), 1)
        ystat[y] = jnp.where(lane2 < 64, plane_top, plane_total)

        def ystat_copy(k):
            return remote(ystat.at[y], ystat.at[y], yst_s, yst_r, along_y(k))

        for k in (2, 1, 3):
            ystat_copy(k).start()

    with jax.named_scope("soft2"):
        lax.fori_loop(3, 4, soften, 0)

    def y_copy(p, k):
        return remote(
            ybuf.at[p, y], ybuf.at[p, y], y_s, y_r.at[p], along_y(k)
        )

    def o_copy(p, k):
        return remote(
            obuf.at[p, y], obuf.at[p, y], o_s, o_r.at[p], along_y(k)
        )

    def gather(p):
        with jax.named_scope(f"sc{p}"):
            drain(recv.at[p, pl.ds(0, XZ - 1)], sc_r.at[p])
            mine = slice(p * PR, (p + 1) * PR)
            acc = jnp.zeros((PR, D), F32)
            for q in range(XZ):
                acc = acc + flipped[mine, q : q + 1] * recv[p, q].astype(F32)
            ybuf[p, y] = acc.astype(BF16)
            for k in (2, 1, 3):
                y_copy(p, k).start()

    def expert(p):
        with jax.named_scope(f"ffn{p}"):
            drain(recv.at[p, pl.ds(0, 3)], y_r.at[p])
            mine = slice(p * PR, (p + 1) * PR)
            acc = jnp.zeros((PR, D), F32)
            for n in range(NY):
                acc = acc + scale[n][mine] * ybuf[p, n].astype(F32)
            hidden = jax.nn.gelu(dot(acc.astype(BF16), win[p])).astype(BF16)
            obuf[p, y] = dot(hidden, wout[p]).astype(BF16)
            for k in (2, 1, 3):
                o_copy(p, k).start()

    def soft(i):
        with jax.named_scope(f"soft{i}"):
            soften(i, 0)

    gather(0)
    gather(1)
    soft(4)
    gather(2)
    with jax.named_scope("ystatw"):
        win_copy.wait()
        wout_copy.wait()
        drain(ystat.at[pl.ds(0, 3)], yst_r)
        tops = [ystat[n][:, 0:1] for n in range(NY)]
        all_top = jnp.maximum(jnp.maximum(tops[0], tops[1]), jnp.maximum(tops[2], tops[3]))
        scale = [jnp.exp(tops[n] - all_top) for n in range(NY)]
        grand = jnp.zeros((ROWS, 1), F32)
        for n in range(NY):
            grand = grand + scale[n] * ystat[n][:, 64:65]
        scale = [v / grand for v in scale]

    def spread(p, k):
        block = so.at[p, xz, core]
        return remote(block, block, ag_s, ag_r.at[p, k // NZ], device(where_is(k)))

    def forward(p, dx):
        fx = (x - dx + NX) % NX
        block = so.at[p, pl.ds(fx * NZ, NZ), core]
        return remote(block, block, fw_s, fw_r.at[p // PH], other)

    def arrive(p, dx):
        n = NZ - (1 if dx == 0 else 0)
        drain(so.at[p, pl.ds(0, n), 0], ag_r.at[p, dx])
        forward(p, dx).start()

    def publish(p):
        with jax.named_scope(f"oex{p}"):
            drain(recv.at[p, pl.ds(0, 3)], o_r.at[p])
            so[p, xz, core] = jnp.sum(obuf[p].astype(F32), axis=0).astype(BF16)
            for k in FAR_FIRST:
                spread(p, k).start()

    expert(0)
    gather(3)
    expert(1)
    soft(5)
    expert(2)
    publish(0)
    expert(3)
    publish(1)
    soft(6)
    publish(2)
    soft(7)
    publish(3)

    def mix(i):
        rows = pl.ds(i * MCH, MCH)
        mixed[rows, :] = dot(comb[rows, 0:SH], first[...])

    turns = (0, 1, 3, 2)
    with jax.named_scope("agA"):
        for p in range(PH):
            for dx in turns:
                arrive(p, dx)
        drain(recv.at[pl.ds(0, PH)], fw_r.at[0])
        first[...] = so[0:PH].reshape(SH, D)
    with jax.named_scope("mixA"):
        for i, dx in enumerate(turns):
            mix(i)
            if i < 2:
                arrive(2, turns[2 * i])
                arrive(2, turns[2 * i + 1])
            else:
                arrive(3, turns[2 * i - 4])
                arrive(3, turns[2 * i - 3])
    with jax.named_scope("agB"):
        drain(recv.at[pl.ds(0, PH)], fw_r.at[1])
        last[...] = so[PH:PIPE].reshape(SH, D)

    with jax.named_scope("ends"):
        drain(stats_recv.at[pl.ds(0, XZ - 1)], st_s)
        drain(recv.at[:, pl.ds(0, XZ - 1)], sc_s)
        drain(ystat.at[pl.ds(0, 3)], yst_s)
        drain(recv.at[:, pl.ds(0, 3)], y_s)
        drain(recv.at[:, pl.ds(0, 3)], o_s)
        drain(recv.at[:, pl.ds(0, XZ - 1)], ag_s)
        drain(recv, fw_s)


def finish_kernel(mixed, comb, last, out, stage, sems):
    def out_copy(i):
        rows = pl.ds(i * SOFT, SOFT)
        return pltpu.make_async_copy(stage.at[rows], out.at[rows], sems.at[i])

    for i in range(TOK // SOFT):
        rows = pl.ds(i * SOFT, SOFT)
        stage[rows, :] = (mixed[rows, :] + dot(comb[rows, SH:S], last[...])).astype(BF16)
        out_copy(i).start()
    for i in range(TOK // SOFT):
        out_copy(i).wait()


def shards(tokens, slot_params, expert_in, expert_out):
    dma, vmem = pltpu.SemaphoreType.DMA, pltpu.VMEM
    operands = [
        pltpu.with_memory_space_constraint(v, pltpu.HBM)
        for v in (tokens, slot_params, expert_in, expert_out)
    ]
    held = pl.pallas_call(
        layer_kernel,
        out_shape=(vmem((TOK, D), F32), vmem((TOK, S), BF16), vmem((SH, D), BF16)),
        in_specs=[pl.BlockSpec(memory_space=pltpu.HBM)] * 4,
        out_specs=[pl.BlockSpec(memory_space=pltpu.VMEM)] * 3,
        scratch_shapes=[
            vmem((TOK, D), BF16),
            vmem((D, S), BF16),
            vmem((4, D, H), BF16),
            vmem((4, H, D), BF16),
            vmem((TOK, S), F32),
            vmem((2, SH, TOK), BF16),
            vmem((S, S), BF16),
            vmem((2, XZ, HR, D), F32),
            vmem((2, XZ, HR, D), BF16),
            vmem((2, XZ, HR, D), BF16),
            vmem((PIPE, XZ, PR, D), BF16),
            vmem((PIPE, XZ, PR, D), BF16),
            vmem((8, S), F32),
            vmem((8, S), F32),
            vmem((S // ROWS, 1, 128), F32),
            vmem((XZ, 1, 128), F32),
            vmem((NY, ROWS, 128), F32),
            vmem((PIPE, NY, PR, D), BF16),
            vmem((PIPE, NY, PR, D), BF16),
            vmem((PIPE, XZ, NC, PR, D), BF16),
            vmem((SH, D), BF16),
            dma((NT + 1,)),
            dma((2,)),
            dma, dma,
            dma((2,)), dma((2,)),
            dma, dma,
            dma, dma((PIPE,)),
            dma, dma,
            dma, dma((PIPE,)),
            dma, dma((PIPE,)),
            dma, dma((PIPE, NX)),
            dma, dma((2,)),
        ],
        compiler_params=pltpu.CompilerParams(
            collective_id=0, has_side_effects=True, vmem_limit_bytes=48 * 1024 * 1024
        ),
        name="layer",
    )(*operands)
    return pl.pallas_call(
        finish_kernel,
        out_shape=jax.ShapeDtypeStruct((TOK, D), BF16),
        in_specs=[pl.BlockSpec(memory_space=pltpu.VMEM)] * 3,
        out_specs=pl.BlockSpec(memory_space=pl.ANY),
        scratch_shapes=[vmem((TOK, D), BF16), dma((TOK // SOFT,))],
        compiler_params=pltpu.CompilerParams(vmem_limit_bytes=32 * 1024 * 1024),
        name="finish",
    )(*held)


def solution(mesh):
    return jax.shard_map(
        shards,
        mesh=mesh,
        in_specs=(
            P(("wide", "narrow"), None),
            P(),
            P("wide", None, "narrow"),
            P("wide", "narrow", None),
        ),
        out_specs=P(("wide", "narrow"), None),
        check_vma=False,
    )
```

```python
import jax
import jax.numpy as jnp
from jax import lax
from jax.experimental import pallas as pl
from jax.experimental.pallas import tpu as pltpu
from jax.sharding import PartitionSpec as P

MESH = pl.DeviceIdType.MESH
F32, BF16 = jnp.float32, jnp.bfloat16
NX, NZ, NY, NC = 4, 4, 4, 2
XZ = NX * NZ
ROWS = 16
PIPE = 4
PR = ROWS // PIPE
PH = PIPE // 2
HR = ROWS // 2
TOK, D, S, H = 2048, 1024, 512, 1024
SP = S // PIPE
SH = S // 2
TCH = 512
NT = TOK // TCH
MCH = 512
FAR_FIRST = (10, 9, 6, 11, 14, 5, 7, 13, 15, 8, 2, 4, 1, 12, 3)
SOFT = 256


def dot(a, b):
    return jnp.dot(a, b, preferred_element_type=F32)


def layer_kernel(
    tok_hbm, par_hbm, win_hbm, wout_hbm, mixed, comb, last,
    tok, par, win, wout, logits, disp_t, order, own, give, part, outb, recv,
    core_own, core_other, stats, stats_recv, ystat, ybuf, obuf, so, first,
    in_sem, w_sem, core_s, core_r, part_s, part_r, st_s, st_r, sc_s, sc_r,
    yst_s, yst_r, y_s, y_r, o_s, o_r, ag_s, ag_r, fw_s, fw_r,
):
    wide = lax.axis_index("wide")
    y = lax.axis_index("narrow")
    core = wide % NC
    xz = wide // NC
    x, z = xz // NZ, xz % NZ

    def where_is(k):
        dx, dz = k // NZ, k % NZ
        return ((x + dx) % NX) * NZ + (z + dz) % NZ

    def device(to_xz):
        return {"wide": to_xz * NC + core, "narrow": y}

    def along_y(k):
        return {"wide": wide, "narrow": (y + k) % NY}

    other = {"wide": xz * NC + 1 - core, "narrow": y}

    def remote(src, dst, send, recv_sem, to):
        return pltpu.make_async_remote_copy(
            src_ref=src, dst_ref=dst, send_sem=send, recv_sem=recv_sem,
            device_id=to, device_id_type=MESH,
        )

    def drain(ref, sem):
        pltpu.make_async_copy(ref, ref, sem).wait()

    def tok_copy(i):
        rows = pl.ds(i * TCH, TCH)
        return pltpu.make_async_copy(tok_hbm.at[rows], tok.at[rows], in_sem.at[i])

    par_copy = pltpu.make_async_copy(par_hbm, par, in_sem.at[NT])
    for i in range(4):
        rows = pl.ds(i * (D // 4), D // 4)
        pltpu.make_async_copy(par_hbm.at[rows], par.at[rows], in_sem.at[NT]).start()
        rows = pl.ds(i * (TCH // 4), TCH // 4)
        pltpu.make_async_copy(tok_hbm.at[rows], tok.at[rows], in_sem.at[0]).start()

    barrier = pltpu.get_barrier_semaphore()

    def greet(to):
        pl.semaphore_signal(barrier, inc=1, device_id=to, device_id_type=MESH)

    greet(other)
    for k in range(1, NY):
        greet(along_y(k))
    for k in range(1, XZ):
        greet(device(where_is(k)))
    for i in range(1, NT):
        tok_copy(i).start()

    with jax.named_scope("logits"):
        par_copy.wait()

        def logits_step(i, peak):
            tok_copy(i).wait()
            rows = pl.ds(pl.multiple_of(i * TCH, TCH), TCH)
            block = dot(tok[rows, :], par[...])
            logits[rows, :] = block
            return jnp.maximum(peak, jnp.max(block, axis=0, keepdims=True))

        peak = lax.fori_loop(0, NT, logits_step, jnp.full((1, S), -jnp.inf, F32))
        win_copy = pltpu.make_async_copy(win_hbm, win, w_sem.at[0])
        wout_copy = pltpu.make_async_copy(wout_hbm, wout, w_sem.at[1])
        win_copy.start()
        wout_copy.start()

    def weigh(i):
        rows = pl.ds(i * MCH, MCH)
        w = jnp.exp(logits[rows, :] - peak)
        turned = jnp.transpose(w).reshape(S // ROWS, 2, HR, MCH)
        for h in range(2):
            disp_t[h, :, rows] = turned[:, h].reshape(SH, MCH).astype(BF16)
        return jnp.sum(w, axis=0, keepdims=True)

    with jax.named_scope("exps"):
        total = weigh(0)
        block = None
        for i in range(TOK // MCH):
            rows = pl.ds(i * MCH, MCH)
            step = dot(disp_t[0, :, rows], tok[rows, :])
            block = step if block is None else block + step
            if i + 1 < TOK // MCH:
                total = total + weigh(i + 1)
        row8 = lax.broadcasted_iota(jnp.int32, (8, S), 0)
        core_own[...] = jnp.where(row8 == 0, peak, total)

    with jax.named_scope("barrier"):
        pl.semaphore_wait(barrier, XZ - 1 + NY - 1 + 1)
        core_copy = remote(core_own, core_other, core_s, core_r, other)
        core_copy.start()

    def part_copy(h):
        return remote(give.at[h], part.at[h], part_s.at[h], part_r.at[h], other)

    def share_block(h, block):
        block = block.reshape(XZ, NC, HR, D)
        own[h] = jnp.where(core == 0, block[:, 0], block[:, 1])
        give[h] = jnp.where(core == 0, block[:, 1], block[:, 0])
        part_copy(h).start()

    with jax.named_scope("mm0"):
        share_block(0, block)

    with jax.named_scope("mm1"):
        share_block(1, dot(disp_t[1], tok[...]))

    with jax.named_scope("stats"):
        core_copy.wait()
        peak_o, total_o = core_other[0:1, :], core_other[1:2, :]
        chip_peak = jnp.maximum(peak, peak_o)
        f_own, f_other = jnp.exp(peak - chip_peak), jnp.exp(peak_o - chip_peak)
        chip_total = f_own * total + f_other * total_o
        turned = jnp.transpose(
            jnp.concatenate(
                [jnp.broadcast_to(v, (32, S)) for v in (f_own, f_other, chip_peak, chip_total)], axis=0
            )
        ).reshape(S // ROWS, ROWS, 128)
        lane = lax.broadcasted_iota(jnp.int32, (S // ROWS, ROWS, 128), 2)
        row = lax.broadcasted_iota(jnp.int32, (S // ROWS, ROWS, 128), 1)
        packed = jnp.where(lane == row, turned[:, :, 64:65], 0.0)
        packed = packed + jnp.where(lane == row + ROWS, turned[:, :, 96:97], 0.0)
        stats[...] = jnp.sum(packed, axis=1, keepdims=True)
        turned = turned.reshape(XZ, NC, ROWS, 128)
        factors = jnp.where(core == 0, turned[:, 0], turned[:, 1])

        for k in FAR_FIRST:
            to_xz = where_is(k)
            remote(
                stats.at[to_xz * NC + core], stats_recv.at[xz], st_s, st_r, device(to_xz)
            ).start()
        stats_recv[xz] = stats[wide]

    def send_step(h):
        part_copy(h).wait()
        f = factors[:, h * HR : (h + 1) * HR]
        joined = (f[:, :, 0:1] * own[h] + f[:, :, 32:33] * part[h]).astype(BF16)
        for p in range(h * PH, (h + 1) * PH):
            outb[p] = joined[:, (p % PH) * PR : (p % PH + 1) * PR]
        for p in range(h * PH, (h + 1) * PH):
            for k in FAR_FIRST:
                to_xz = where_is(k)
                remote(
                    outb.at[p, to_xz], recv.at[p, xz], sc_s, sc_r.at[p], device(to_xz)
                ).start()
            recv[p, xz] = outb[p, xz]

    def soften(i, carry):
        rows = pl.ds(pl.multiple_of(i * SOFT, SOFT), SOFT)
        block = logits[rows, :]
        e = jnp.exp(block - jnp.max(block, axis=1, keepdims=True))
        share = (e / jnp.sum(e, axis=1, keepdims=True)).astype(BF16)
        comb[rows, :] = dot(share, order[...]).astype(BF16)
        return carry

    with jax.named_scope("send0"):
        send_step(0)
    with jax.named_scope("send1"):
        send_step(1)
    with jax.named_scope("order"):
        new = lax.broadcasted_iota(jnp.int32, (S, S), 1)
        old = lax.broadcasted_iota(jnp.int32, (S, S), 0)
        within = new % SP
        source = (within // PR) * ROWS + (new // SP) * PR + within % PR
        order[...] = jnp.where(old == source, 1.0, 0.0).astype(BF16)
    with jax.named_scope("soft1"):
        lax.fori_loop(0, 3, soften, 0)

    with jax.named_scope("ystat"):
        drain(stats_recv.at[pl.ds(0, XZ - 1)], st_r)
        got = stats_recv[...].reshape(XZ, 128)
        top = jnp.max(got, axis=0, keepdims=True)
        factor = jnp.exp(jnp.minimum(got - top, 0.0))
        scaled = factor * pltpu.roll(got, 128 - ROWS, 1)
        flipped = jnp.transpose(
            jnp.concatenate([factor, scaled, jnp.broadcast_to(top, (128 - 2 * XZ, 128))], axis=0)
        )[0:ROWS, :]
        plane_top = flipped[:, 2 * XZ : 2 * XZ + 1]
        plane_total = jnp.sum(flipped[:, XZ : 2 * XZ], axis=1, keepdims=True)
        lane2 = lax.broadcasted_iota(jnp.int32, (ROWS, 128), 1)
        ystat[y] = jnp.where(lane2 < 64, plane_top, plane_total)

        def ystat_copy(k):
            return remote(ystat.at[y], ystat.at[y], yst_s, yst_r, along_y(k))

        for k in (2, 1, 3):
            ystat_copy(k).start()

    with jax.named_scope("soft2"):
        lax.fori_loop(3, 4, soften, 0)

    def y_copy(p, k):
        return remote(
            ybuf.at[p, y], ybuf.at[p, y], y_s, y_r.at[p], along_y(k)
        )

    def o_copy(p, k):
        return remote(
            obuf.at[p, y], obuf.at[p, y], o_s, o_r.at[p], along_y(k)
        )

    def gather(p):
        with jax.named_scope(f"sc{p}"):
            drain(recv.at[p, pl.ds(0, XZ - 1)], sc_r.at[p])
            mine = slice(p * PR, (p + 1) * PR)
            acc = jnp.zeros((PR, D), F32)
            for q in range(XZ):
                acc = acc + flipped[mine, q : q + 1] * recv[p, q].astype(F32)
            ybuf[p, y] = acc.astype(BF16)
            for k in (2, 1, 3):
                y_copy(p, k).start()

    def expert(p):
        with jax.named_scope(f"ffn{p}"):
            drain(recv.at[p, pl.ds(0, 3)], y_r.at[p])
            mine = slice(p * PR, (p + 1) * PR)
            acc = jnp.zeros((PR, D), F32)
            for n in range(NY):
                acc = acc + scale[n][mine] * ybuf[p, n].astype(F32)
            hidden = jax.nn.gelu(dot(acc.astype(BF16), win[p])).astype(BF16)
            obuf[p, y] = dot(hidden, wout[p]).astype(BF16)
            for k in (2, 1, 3):
                o_copy(p, k).start()

    def soft(i):
        with jax.named_scope(f"soft{i}"):
            soften(i, 0)

    gather(0)
    gather(1)
    soft(4)
    gather(2)
    with jax.named_scope("ystatw"):
        win_copy.wait()
        wout_copy.wait()
        drain(ystat.at[pl.ds(0, 3)], yst_r)
        tops = [ystat[n][:, 0:1] for n in range(NY)]
        all_top = jnp.maximum(jnp.maximum(tops[0], tops[1]), jnp.maximum(tops[2], tops[3]))
        scale = [jnp.exp(tops[n] - all_top) for n in range(NY)]
        grand = jnp.zeros((ROWS, 1), F32)
        for n in range(NY):
            grand = grand + scale[n] * ystat[n][:, 64:65]
        scale = [v / grand for v in scale]

    def spread(p, k):
        block = so.at[p, xz, core]
        return remote(block, block, ag_s, ag_r.at[p if p < PIPE - 1 else p + k // NZ], device(where_is(k)))

    def forward(p, dx):
        fx = (x - dx + NX) % NX
        block = so.at[p, pl.ds(fx * NZ, NZ), core]
        return remote(block, block, fw_s, fw_r.at[p // PH], other)

    def arrive(p):
        drain(recv.at[p, pl.ds(0, XZ - 1)], ag_r.at[p])
        block = so.at[p, :, core]
        remote(block, block, fw_s, fw_r.at[p // PH], other).start()

    def arrive_row(p, dx):
        drain(so.at[p, pl.ds(0, NZ - (1 if dx == 0 else 0)), 0], ag_r.at[p + dx])
        forward(p, dx).start()

    def publish(p):
        with jax.named_scope(f"oex{p}"):
            drain(recv.at[p, pl.ds(0, 3)], o_r.at[p])
            so[p, xz, core] = jnp.sum(obuf[p].astype(F32), axis=0).astype(BF16)
            for k in FAR_FIRST:
                spread(p, k).start()

    expert(0)
    gather(3)
    expert(1)
    soft(5)
    expert(2)
    publish(0)
    expert(3)
    publish(1)
    soft(6)
    publish(2)
    soft(7)
    publish(3)

    def mix(i):
        rows = pl.ds(i * MCH, MCH)
        mixed[rows, :] = dot(comb[rows, 0:SH], first[...])

    turns = (0, 1, 3, 2)
    with jax.named_scope("agA"):
        for p in range(PH):
            arrive(p)
        drain(recv.at[pl.ds(0, PH)], fw_r.at[0])
        first[...] = so[0:PH].reshape(SH, D)
    with jax.named_scope("mixA"):
        mix(0)
        mix(1)
        arrive(2)
        mix(2)
        for dx in turns:
            arrive_row(3, dx)
        mix(3)
    with jax.named_scope("agB"):
        drain(recv.at[pl.ds(0, PH)], fw_r.at[1])
        last[...] = so[PH:PIPE].reshape(SH, D)

    with jax.named_scope("ends"):
        drain(stats_recv.at[pl.ds(0, XZ - 1)], st_s)
        drain(recv.at[:, pl.ds(0, XZ - 1)], sc_s)
        drain(ystat.at[pl.ds(0, 3)], yst_s)
        drain(recv.at[:, pl.ds(0, 3)], y_s)
        drain(recv.at[:, pl.ds(0, 3)], o_s)
        drain(recv.at[:, pl.ds(0, XZ - 1)], ag_s)
        drain(recv, fw_s)


def finish_kernel(mixed, comb, last, out, stage, sems):
    def out_copy(i):
        rows = pl.ds(i * SOFT, SOFT)
        return pltpu.make_async_copy(stage.at[rows], out.at[rows], sems.at[i])

    for i in range(TOK // SOFT):
        rows = pl.ds(i * SOFT, SOFT)
        stage[rows, :] = (mixed[rows, :] + dot(comb[rows, SH:S], last[...])).astype(BF16)
        out_copy(i).start()
    for i in range(TOK // SOFT):
        out_copy(i).wait()


def shards(tokens, slot_params, expert_in, expert_out):
    dma, vmem = pltpu.SemaphoreType.DMA, pltpu.VMEM
    operands = [
        pltpu.with_memory_space_constraint(v, pltpu.HBM)
        for v in (tokens, slot_params, expert_in, expert_out)
    ]
    held = pl.pallas_call(
        layer_kernel,
        out_shape=(vmem((TOK, D), F32), vmem((TOK, S), BF16), vmem((SH, D), BF16)),
        in_specs=[pl.BlockSpec(memory_space=pltpu.HBM)] * 4,
        out_specs=[pl.BlockSpec(memory_space=pltpu.VMEM)] * 3,
        scratch_shapes=[
            vmem((TOK, D), BF16),
            vmem((D, S), BF16),
            vmem((4, D, H), BF16),
            vmem((4, H, D), BF16),
            vmem((TOK, S), F32),
            vmem((2, SH, TOK), BF16),
            vmem((S, S), BF16),
            vmem((2, XZ, HR, D), F32),
            vmem((2, XZ, HR, D), F32),
            vmem((2, XZ, HR, D), F32),
            vmem((PIPE, XZ, PR, D), BF16),
            vmem((PIPE, XZ, PR, D), BF16),
            vmem((8, S), F32),
            vmem((8, S), F32),
            vmem((S // ROWS, 1, 128), F32),
            vmem((XZ, 1, 128), F32),
            vmem((NY, ROWS, 128), F32),
            vmem((PIPE, NY, PR, D), BF16),
            vmem((PIPE, NY, PR, D), BF16),
            vmem((PIPE, XZ, NC, PR, D), BF16),
            vmem((SH, D), BF16),
            dma((NT + 1,)),
            dma((2,)),
            dma, dma,
            dma((2,)), dma((2,)),
            dma, dma,
            dma, dma((PIPE,)),
            dma, dma,
            dma, dma((PIPE,)),
            dma, dma((PIPE,)),
            dma, dma((PIPE - 1 + NX,)),
            dma, dma((2,)),
        ],
        compiler_params=pltpu.CompilerParams(
            collective_id=0, has_side_effects=True, vmem_limit_bytes=48 * 1024 * 1024
        ),
        name="layer",
    )(*operands)
    return pl.pallas_call(
        finish_kernel,
        out_shape=jax.ShapeDtypeStruct((TOK, D), BF16),
        in_specs=[pl.BlockSpec(memory_space=pltpu.VMEM)] * 3,
        out_specs=pl.BlockSpec(memory_space=pl.ANY),
        scratch_shapes=[vmem((TOK, D), BF16), dma((TOK // SOFT,))],
        compiler_params=pltpu.CompilerParams(vmem_limit_bytes=32 * 1024 * 1024),
        name="finish",
    )(*held)


def solution(mesh):
    return jax.shard_map(
        shards,
        mesh=mesh,
        in_specs=(
            P(("wide", "narrow"), None),
            P(),
            P("wide", None, "narrow"),
            P("wide", "narrow", None),
        ),
        out_specs=P(("wide", "narrow"), None),
        check_vma=False,
    )
```

```python
import jax
import jax.numpy as jnp
from jax import lax
from jax.experimental import pallas as pl
from jax.experimental.pallas import tpu as pltpu
from jax.sharding import PartitionSpec as P

MESH = pl.DeviceIdType.MESH
F32, BF16 = jnp.float32, jnp.bfloat16
NX, NZ, NY, NC = 4, 4, 4, 2
XZ = NX * NZ
ROWS = 16
PIPE = 4
PR = ROWS // PIPE
PH = PIPE // 2
HR = ROWS // 2
TOK, D, S, H = 2048, 1024, 512, 1024
SP = S // PIPE
SH = S // 2
TCH = 512
NT = TOK // TCH
MCH = 512
FAR_FIRST = (10, 9, 6, 11, 14, 5, 7, 13, 15, 8, 2, 4, 1, 12, 3)
SOFT = 256


def dot(a, b):
    return jnp.dot(a, b, preferred_element_type=F32)


def layer_kernel(
    tok_hbm, par_hbm, win_hbm, wout_hbm, mixed, comb, last,
    tok, par, win, wout, logits, disp_t, order, own, give, part, outb, recv,
    core_own, core_other, stats, stats_recv, ystat, ybuf, obuf, so, first,
    in_sem, w_sem, core_s, core_r, part_s, part_r, st_s, st_r, sc_s, sc_r,
    yst_s, yst_r, y_s, y_r, o_s, o_r, ag_s, ag_r, fw_s, fw_r,
):
    wide = lax.axis_index("wide")
    y = lax.axis_index("narrow")
    core = wide % NC
    xz = wide // NC
    x, z = xz // NZ, xz % NZ

    def where_is(k):
        dx, dz = k // NZ, k % NZ
        return ((x + dx) % NX) * NZ + (z + dz) % NZ

    def device(to_xz):
        return {"wide": to_xz * NC + core, "narrow": y}

    def along_y(k):
        return {"wide": wide, "narrow": (y + k) % NY}

    other = {"wide": xz * NC + 1 - core, "narrow": y}

    def remote(src, dst, send, recv_sem, to):
        return pltpu.make_async_remote_copy(
            src_ref=src, dst_ref=dst, send_sem=send, recv_sem=recv_sem,
            device_id=to, device_id_type=MESH,
        )

    def drain(ref, sem):
        pltpu.make_async_copy(ref, ref, sem).wait()

    def tok_copy(i):
        rows = pl.ds(i * TCH, TCH)
        return pltpu.make_async_copy(tok_hbm.at[rows], tok.at[rows], in_sem.at[i])

    par_copy = pltpu.make_async_copy(par_hbm, par, in_sem.at[NT])
    for i in range(4):
        rows = pl.ds(i * (D // 4), D // 4)
        pltpu.make_async_copy(par_hbm.at[rows], par.at[rows], in_sem.at[NT]).start()
        rows = pl.ds(i * (TCH // 4), TCH // 4)
        pltpu.make_async_copy(tok_hbm.at[rows], tok.at[rows], in_sem.at[0]).start()

    barrier = pltpu.get_barrier_semaphore()

    def greet(to):
        pl.semaphore_signal(barrier, inc=1, device_id=to, device_id_type=MESH)

    greet(other)
    for k in range(1, NY):
        greet(along_y(k))
    for k in range(1, XZ):
        greet(device(where_is(k)))
    for i in range(1, NT):
        tok_copy(i).start()

    with jax.named_scope("logits"):
        par_copy.wait()

        def logits_step(i, peak):
            tok_copy(i).wait()
            rows = pl.ds(pl.multiple_of(i * TCH, TCH), TCH)
            block = dot(tok[rows, :], par[...])
            logits[rows, :] = block
            return jnp.maximum(peak, jnp.max(block, axis=0, keepdims=True))

        peak = lax.fori_loop(0, NT, logits_step, jnp.full((1, S), -jnp.inf, F32))
        win_copy = pltpu.make_async_copy(win_hbm, win, w_sem.at[0])
        wout_copy = pltpu.make_async_copy(wout_hbm, wout, w_sem.at[1])
        win_copy.start()
        wout_copy.start()

    def weigh(i):
        rows = pl.ds(i * MCH, MCH)
        w = jnp.exp(logits[rows, :] - peak)
        turned = jnp.transpose(w).reshape(S // ROWS, 2, HR, MCH)
        for h in range(2):
            disp_t[h, :, rows] = turned[:, h].reshape(SH, MCH).astype(BF16)
        return jnp.sum(w, axis=0, keepdims=True)

    with jax.named_scope("exps"):
        total = weigh(0)
        block = None
        for i in range(TOK // MCH):
            rows = pl.ds(i * MCH, MCH)
            step = dot(disp_t[0, :, rows], tok[rows, :])
            block = step if block is None else block + step
            if i + 1 < TOK // MCH:
                total = total + weigh(i + 1)
        row8 = lax.broadcasted_iota(jnp.int32, (8, S), 0)
        core_own[...] = jnp.where(row8 == 0, peak, total)

    with jax.named_scope("barrier"):
        pl.semaphore_wait(barrier, XZ - 1 + NY - 1 + 1)
        core_copy = remote(core_own, core_other, core_s, core_r, other)
        core_copy.start()

    def part_copy(h):
        return remote(give.at[h], part.at[h], part_s.at[h], part_r.at[h], other)

    def share_block(h, block):
        block = block.reshape(XZ, NC, HR, D)
        own[h] = jnp.where(core == 0, block[:, 0], block[:, 1])
        give[h] = jnp.where(core == 0, block[:, 1], block[:, 0]).astype(BF16)
        part_copy(h).start()

    with jax.named_scope("mm0"):
        share_block(0, block)

    def stash(lo):
        cols = slice(lo, lo + D // 2)
        block = dot(disp_t[1], tok[:, cols]).reshape(XZ, NC, HR, D // 2)
        own[1, :, :, cols] = jnp.where(core == 0, block[:, 0], block[:, 1])
        give[1, :, :, cols] = jnp.where(core == 0, block[:, 1], block[:, 0]).astype(BF16)

    with jax.named_scope("mm1"):
        stash(0)

    with jax.named_scope("stats"):
        core_copy.wait()
        peak_o, total_o = core_other[0:1, :], core_other[1:2, :]
        chip_peak = jnp.maximum(peak, peak_o)
        f_own, f_other = jnp.exp(peak - chip_peak), jnp.exp(peak_o - chip_peak)
        chip_total = f_own * total + f_other * total_o
        turned = jnp.transpose(
            jnp.concatenate(
                [jnp.broadcast_to(v, (32, S)) for v in (f_own, f_other, chip_peak, chip_total)], axis=0
            )
        ).reshape(S // ROWS, ROWS, 128)
        lane = lax.broadcasted_iota(jnp.int32, (S // ROWS, ROWS, 128), 2)
        row = lax.broadcasted_iota(jnp.int32, (S // ROWS, ROWS, 128), 1)
        packed = jnp.where(lane == row, turned[:, :, 64:65], 0.0)
        packed = packed + jnp.where(lane == row + ROWS, turned[:, :, 96:97], 0.0)
        stats[...] = jnp.sum(packed, axis=1, keepdims=True)
        turned = turned.reshape(XZ, NC, ROWS, 128)
        factors = jnp.where(core == 0, turned[:, 0], turned[:, 1])

        for k in FAR_FIRST:
            to_xz = where_is(k)
            remote(
                stats.at[to_xz * NC + core], stats_recv.at[xz], st_s, st_r, device(to_xz)
            ).start()
        stats_recv[xz] = stats[wide]

    def send_step(h):
        part_copy(h).wait()
        f = factors[:, h * HR : (h + 1) * HR]
        joined = (f[:, :, 0:1] * own[h] + f[:, :, 32:33] * part[h].astype(F32)).astype(BF16)
        for p in range(h * PH, (h + 1) * PH):
            outb[p] = joined[:, (p % PH) * PR : (p % PH + 1) * PR]
        for p in range(h * PH, (h + 1) * PH):
            for k in FAR_FIRST:
                to_xz = where_is(k)
                remote(
                    outb.at[p, to_xz], recv.at[p, xz], sc_s, sc_r.at[p], device(to_xz)
                ).start()
            recv[p, xz] = outb[p, xz]

    def soften(i, carry):
        rows = pl.ds(pl.multiple_of(i * SOFT, SOFT), SOFT)
        block = logits[rows, :]
        e = jnp.exp(block - jnp.max(block, axis=1, keepdims=True))
        share = (e / jnp.sum(e, axis=1, keepdims=True)).astype(BF16)
        comb[rows, :] = dot(share, order[...]).astype(BF16)
        return carry

    with jax.named_scope("send0"):
        send_step(0)
    with jax.named_scope("mm2"):
        stash(D // 2)
        part_copy(1).start()
    with jax.named_scope("order"):
        new = lax.broadcasted_iota(jnp.int32, (S, S), 1)
        old = lax.broadcasted_iota(jnp.int32, (S, S), 0)
        within = new % SP
        source = (within // PR) * ROWS + (new // SP) * PR + within % PR
        order[...] = jnp.where(old == source, 1.0, 0.0).astype(BF16)
    with jax.named_scope("soft1"):
        lax.fori_loop(0, 1, soften, 0)
    with jax.named_scope("send1"):
        send_step(1)
    with jax.named_scope("soft1b"):
        lax.fori_loop(1, 3, soften, 0)

    with jax.named_scope("ystat"):
        drain(stats_recv.at[pl.ds(0, XZ - 1)], st_r)
        got = stats_recv[...].reshape(XZ, 128)
        top = jnp.max(got, axis=0, keepdims=True)
        factor = jnp.exp(jnp.minimum(got - top, 0.0))
        scaled = factor * pltpu.roll(got, 128 - ROWS, 1)
        flipped = jnp.transpose(
            jnp.concatenate([factor, scaled, jnp.broadcast_to(top, (128 - 2 * XZ, 128))], axis=0)
        )[0:ROWS, :]
        plane_top = flipped[:, 2 * XZ : 2 * XZ + 1]
        plane_total = jnp.sum(flipped[:, XZ : 2 * XZ], axis=1, keepdims=True)
        lane2 = lax.broadcasted_iota(jnp.int32, (ROWS, 128), 1)
        ystat[y] = jnp.where(lane2 < 64, plane_top, plane_total)

        def ystat_copy(k):
            return remote(ystat.at[y], ystat.at[y], yst_s, yst_r, along_y(k))

        for k in (2, 1, 3):
            ystat_copy(k).start()

    with jax.named_scope("soft2"):
        lax.fori_loop(3, 4, soften, 0)

    def y_copy(p, k):
        return remote(
            ybuf.at[p, y], ybuf.at[p, y], y_s, y_r.at[p], along_y(k)
        )

    def o_copy(p, k):
        return remote(
            obuf.at[p, y], obuf.at[p, y], o_s, o_r.at[p], along_y(k)
        )

    def gather(p):
        with jax.named_scope(f"sc{p}"):
            drain(recv.at[p, pl.ds(0, XZ - 1)], sc_r.at[p])
            mine = slice(p * PR, (p + 1) * PR)
            acc = jnp.zeros((PR, D), F32)
            for q in range(XZ):
                acc = acc + flipped[mine, q : q + 1] * recv[p, q].astype(F32)
            ybuf[p, y] = acc.astype(BF16)
            for k in (2, 1, 3):
                y_copy(p, k).start()

    def expert(p):
        with jax.named_scope(f"ffn{p}"):
            drain(recv.at[p, pl.ds(0, 3)], y_r.at[p])
            mine = slice(p * PR, (p + 1) * PR)
            acc = jnp.zeros((PR, D), F32)
            for n in range(NY):
                acc = acc + scale[n][mine] * ybuf[p, n].astype(F32)
            hidden = jax.nn.gelu(dot(acc.astype(BF16), win[p])).astype(BF16)
            obuf[p, y] = dot(hidden, wout[p]).astype(BF16)
            for k in (2, 1, 3):
                o_copy(p, k).start()

    def soft(i):
        with jax.named_scope(f"soft{i}"):
            soften(i, 0)

    gather(0)
    gather(1)
    soft(4)
    gather(2)
    with jax.named_scope("ystatw"):
        win_copy.wait()
        wout_copy.wait()
        drain(ystat.at[pl.ds(0, 3)], yst_r)
        tops = [ystat[n][:, 0:1] for n in range(NY)]
        all_top = jnp.maximum(jnp.maximum(tops[0], tops[1]), jnp.maximum(tops[2], tops[3]))
        scale = [jnp.exp(tops[n] - all_top) for n in range(NY)]
        grand = jnp.zeros((ROWS, 1), F32)
        for n in range(NY):
            grand = grand + scale[n] * ystat[n][:, 64:65]
        scale = [v / grand for v in scale]

    def spread(p, k):
        block = so.at[p, xz, core]
        return remote(block, block, ag_s, ag_r.at[p if p < PIPE - 1 else p + k // NZ], device(where_is(k)))

    def forward(p, dx):
        fx = (x - dx + NX) % NX
        block = so.at[p, pl.ds(fx * NZ, NZ), core]
        return remote(block, block, fw_s, fw_r.at[p // PH], other)

    def arrive(p):
        drain(recv.at[p, pl.ds(0, XZ - 1)], ag_r.at[p])
        block = so.at[p, :, core]
        remote(block, block, fw_s, fw_r.at[p // PH], other).start()

    def arrive_row(p, dx):
        drain(so.at[p, pl.ds(0, NZ - (1 if dx == 0 else 0)), 0], ag_r.at[p + dx])
        forward(p, dx).start()

    def publish(p):
        with jax.named_scope(f"oex{p}"):
            drain(recv.at[p, pl.ds(0, 3)], o_r.at[p])
            so[p, xz, core] = jnp.sum(obuf[p].astype(F32), axis=0).astype(BF16)
            for k in FAR_FIRST:
                spread(p, k).start()

    expert(0)
    gather(3)
    expert(1)
    soft(5)
    expert(2)
    publish(0)
    expert(3)
    publish(1)
    soft(6)
    publish(2)
    soft(7)
    publish(3)

    def mix(i):
        rows = pl.ds(i * MCH, MCH)
        mixed[rows, :] = dot(comb[rows, 0:SH], first[...])

    turns = (0, 1, 3, 2)
    with jax.named_scope("agA"):
        for p in range(PH):
            arrive(p)
        drain(recv.at[pl.ds(0, PH)], fw_r.at[0])
        first[...] = so[0:PH].reshape(SH, D)
    with jax.named_scope("mixA"):
        mix(0)
        mix(1)
        arrive(2)
        mix(2)
        for dx in turns:
            arrive_row(3, dx)
        mix(3)
    with jax.named_scope("agB"):
        drain(recv.at[pl.ds(0, PH)], fw_r.at[1])
        last[...] = so[PH:PIPE].reshape(SH, D)

    with jax.named_scope("ends"):
        drain(stats_recv.at[pl.ds(0, XZ - 1)], st_s)
        drain(recv.at[:, pl.ds(0, XZ - 1)], sc_s)
        drain(ystat.at[pl.ds(0, 3)], yst_s)
        drain(recv.at[:, pl.ds(0, 3)], y_s)
        drain(recv.at[:, pl.ds(0, 3)], o_s)
        drain(recv.at[:, pl.ds(0, XZ - 1)], ag_s)
        drain(recv, fw_s)


def finish_kernel(mixed, comb, last, out, stage, sems):
    def out_copy(i):
        rows = pl.ds(i * SOFT, SOFT)
        return pltpu.make_async_copy(stage.at[rows], out.at[rows], sems.at[i])

    for i in range(TOK // SOFT):
        rows = pl.ds(i * SOFT, SOFT)
        stage[rows, :] = (mixed[rows, :] + dot(comb[rows, SH:S], last[...])).astype(BF16)
        out_copy(i).start()
    for i in range(TOK // SOFT):
        out_copy(i).wait()


def shards(tokens, slot_params, expert_in, expert_out):
    dma, vmem = pltpu.SemaphoreType.DMA, pltpu.VMEM
    operands = [
        pltpu.with_memory_space_constraint(v, pltpu.HBM)
        for v in (tokens, slot_params, expert_in, expert_out)
    ]
    held = pl.pallas_call(
        layer_kernel,
        out_shape=(vmem((TOK, D), F32), vmem((TOK, S), BF16), vmem((SH, D), BF16)),
        in_specs=[pl.BlockSpec(memory_space=pltpu.HBM)] * 4,
        out_specs=[pl.BlockSpec(memory_space=pltpu.VMEM)] * 3,
        scratch_shapes=[
            vmem((TOK, D), BF16),
            vmem((D, S), BF16),
            vmem((4, D, H), BF16),
            vmem((4, H, D), BF16),
            vmem((TOK, S), F32),
            vmem((2, SH, TOK), BF16),
            vmem((S, S), BF16),
            vmem((2, XZ, HR, D), F32),
            vmem((2, XZ, HR, D), BF16),
            vmem((2, XZ, HR, D), BF16),
            vmem((PIPE, XZ, PR, D), BF16),
            vmem((PIPE, XZ, PR, D), BF16),
            vmem((8, S), F32),
            vmem((8, S), F32),
            vmem((S // ROWS, 1, 128), F32),
            vmem((XZ, 1, 128), F32),
            vmem((NY, ROWS, 128), F32),
            vmem((PIPE, NY, PR, D), BF16),
            vmem((PIPE, NY, PR, D), BF16),
            vmem((PIPE, XZ, NC, PR, D), BF16),
            vmem((SH, D), BF16),
            dma((NT + 1,)),
            dma((2,)),
            dma, dma,
            dma((2,)), dma((2,)),
            dma, dma,
            dma, dma((PIPE,)),
            dma, dma,
            dma, dma((PIPE,)),
            dma, dma((PIPE,)),
            dma, dma((PIPE - 1 + NX,)),
            dma, dma((2,)),
        ],
        compiler_params=pltpu.CompilerParams(
            collective_id=0, has_side_effects=True, vmem_limit_bytes=48 * 1024 * 1024
        ),
        name="layer",
    )(*operands)
    return pl.pallas_call(
        finish_kernel,
        out_shape=jax.ShapeDtypeStruct((TOK, D), BF16),
        in_specs=[pl.BlockSpec(memory_space=pltpu.VMEM)] * 3,
        out_specs=pl.BlockSpec(memory_space=pl.ANY),
        scratch_shapes=[vmem((TOK, D), BF16), dma((TOK // SOFT,))],
        compiler_params=pltpu.CompilerParams(vmem_limit_bytes=32 * 1024 * 1024),
        name="finish",
    )(*held)


def solution(mesh):
    return jax.shard_map(
        shards,
        mesh=mesh,
        in_specs=(
            P(("wide", "narrow"), None),
            P(),
            P("wide", None, "narrow"),
            P("wide", "narrow", None),
        ),
        out_specs=P(("wide", "narrow"), None),
        check_vma=False,
    )
```
